1024 devices in a mesh: ctx: 128 (over x, z), fsdp: 8 (over y, core).
Axes of the slice: x: 4, y: 4, z: 32, core: 2. Of those that a mesh axis runs over, the one named last changes fastest.
Arguments:
- query_rows: bfloat16 [16384, 4096], P('ctx', 'fsdp'), may hold values from -6 to 6
- key_rows: bfloat16 [16384, 4096], P('ctx', 'fsdp'), may hold values from -6 to 6
- value_rows: bfloat16 [16384, 4096], P('ctx', 'fsdp'), may hold values from -6 to 6
- filters: float32 [256, 128], P('fsdp'), may hold values from -0.5 to 0.5
- out_weight: bfloat16 [4096, 4096], P('ctx', 'fsdp'), may hold values from -0.09375 to 0.09375
- out_grad: bfloat16 [16384, 4096], P('ctx', 'fsdp'), may hold values from -6 to 6
Outputs:
- mixed_out: bfloat16 [16384, 4096], P('ctx', 'fsdp')
- query_grad: bfloat16 [16384, 4096], P('ctx', 'fsdp')
- key_grad: bfloat16 [16384, 4096], P('ctx', 'fsdp')
- value_grad: bfloat16 [16384, 4096], P('ctx', 'fsdp')
The draws below stay inside these ranges and needn't reach their ends.
All inputs are finite; a program needn't handle non-finite values.
Results may differ from the reference program's by a relative error of at most 0.022.
Values may be sent and summed in bfloat16 or wider, within the bound.
A program may use at most 64 MiB of HBM per device.

```python
import jax
import jax.numpy as jnp
from jax import lax

CH = 4096
DOUT = 4096
TAPS = 128
GROUP = 16
TOKENS = 16384
FILTERS = 256
N_FSDP = 8


def block_scale(key, shape, split, smallest, top_value):
    loudness = 1.0
    for position, parts in split:
        heights = jax.random.uniform(jax.random.fold_in(jax.random.fold_in(key, 6), position), (parts,), jnp.float32, smallest / len(split), top_value / len(split))
        loudness = loudness * jnp.repeat(jnp.exp(heights), shape[position] // parts).reshape((-1,) + (1,) * (len(shape) - 1 - position))
    return loudness


def normal_values(rng, extent, scale, most, split=(), dtype=jnp.bfloat16):
    values = jax.random.normal(rng, extent, jnp.float32) * scale
    if len(split) > 0:
        values = block_scale(rng, extent, split, -0.22, 0.18) * values
    return jnp.clip(values, min=-most, max=most).astype(dtype)


def setup_inputs(seed: int = 0) -> dict:
    keys = jax.random.split(jax.random.key(seed), 7)
    query_rows = normal_values(keys[0], (TOKENS, CH), 1.0, 6.0, ((0, 128), (1, 8)))
    key_rows = normal_values(keys[1], (TOKENS, CH), 1.0, 6.0, ((0, 128), (1, 8)))
    value_rows = normal_values(keys[2], (TOKENS, CH), 1.0, 6.0, ((0, 128), (1, 8)))
    filters = normal_values(keys[3], (FILTERS, TAPS), TAPS ** -0.5, 0.5, ((0, 8),), jnp.float32)
    out_weight = normal_values(keys[4], (CH, DOUT), CH ** -0.5, 0.09375, ((0, 128), (1, 8)))
    out_grad = normal_values(keys[5], (TOKENS, DOUT), 1.0, 6.0, ((0, 128), (1, 8)))
    return {"query_rows": query_rows, "key_rows": key_rows, "value_rows": value_rows, "filters": filters, "out_weight": out_weight, "out_grad": out_grad}


def spread(filters):
    return jnp.repeat(filters, GROUP, axis=0)


def causal_conv(signal, taps_wide):
    length = signal.shape[0]
    padded = jnp.concatenate([jnp.zeros((TAPS - 1, signal.shape[1]), jnp.float32), signal], axis=0)

    def step(lag_index, running):
        lag_value = jnp.asarray(lag_index).astype(jnp.int32)
        window = lax.dynamic_slice_in_dim(padded, (TAPS - 1 - lag_value).astype(jnp.int32), length, 0)
        column = lax.dynamic_slice_in_dim(taps_wide, lag_value, 1, 1)[:, 0]
        return running + window * column[None, :]

    return lax.fori_loop(0, TAPS, step, jnp.zeros_like(signal))


def anti_conv(signal, taps_wide):
    length = signal.shape[0]
    padded = jnp.concatenate([signal, jnp.zeros((TAPS - 1, signal.shape[1]), jnp.float32)], axis=0)

    def step(lag_index, running):
        lag_value = jnp.asarray(lag_index).astype(jnp.int32)
        window = lax.dynamic_slice_in_dim(padded, lag_value, length, 0)
        column = lax.dynamic_slice_in_dim(taps_wide, lag_value, 1, 1)[:, 0]
        return running + window * column[None, :]

    return lax.fori_loop(0, TAPS, step, jnp.zeros_like(signal))


def reference(query_rows, key_rows, value_rows, filters, out_weight, out_grad):
    taps_wide = spread(filters.astype(jnp.float32))
    query_wide = query_rows.astype(jnp.float32)
    key_wide = key_rows.astype(jnp.float32)
    value_wide = value_rows.astype(jnp.float32)
    product = (key_wide * value_wide).astype(jnp.bfloat16)
    conv = causal_conv(product.astype(jnp.float32), taps_wide)
    gated = (query_wide * conv).astype(jnp.bfloat16)
    mixed_out = jnp.dot(gated, out_weight, preferred_element_type=jnp.float32).astype(jnp.bfloat16)
    shard_width = DOUT // N_FSDP
    gate_grad = jnp.zeros((out_grad.shape[0], out_weight.shape[0]), jnp.float32)
    for shard in range(N_FSDP):
        grad_part = out_grad[:, shard * shard_width:(shard + 1) * shard_width]
        weight_part = out_weight[:, shard * shard_width:(shard + 1) * shard_width]
        partial_sum = jnp.dot(grad_part, weight_part.T, preferred_element_type=jnp.float32)
        rounded = lax.optimization_barrier(partial_sum.astype(jnp.bfloat16))
        gate_grad = gate_grad + rounded.astype(jnp.float32)
    conv_grad = (gate_grad * query_wide).astype(jnp.bfloat16)
    query_grad = (gate_grad * conv).astype(jnp.bfloat16)
    product_grad = anti_conv(conv_grad.astype(jnp.float32), taps_wide)
    key_grad = (product_grad * value_wide).astype(jnp.bfloat16)
    value_grad = (product_grad * key_wide).astype(jnp.bfloat16)
    return mixed_out, query_grad, key_grad, value_grad
```

```python
import functools

import jax
import jax.numpy as jnp
from jax import lax
from jax.experimental import pallas as pl
from jax.experimental.pallas import tpu as pltpu
from jax.sharding import PartitionSpec as P

MESH = pl.DeviceIdType.MESH
BF = jnp.bfloat16
F32 = jnp.float32
SUB = 128
X_CHIPS = 4
A_COLS = 384


def kernel(
    X, Z, NF,
    q_hbm, k_hbm, v_hbm, f_hbm, w_hbm, og_hbm,
    mix_o, qg_o, kg_o, vg_o,
    q, k, v, og, filt, w, ext, band_f, band_b, conv, gated, stage, recv, cg, nxt, pg,
    load_sem, own_sem, za_send, xa_send, zb_send, xb_send, za, xr, xrel, zb, xb,
    g_send, g_recv, r_send, r_recv, p_send, p_recv, c_send, c_recv,
):
    C = X * Z
    rows = w_hbm.shape[0]
    CA = A_COLS
    cols = w_hbm.shape[1]
    M = Z // 4
    NG = Z * rows // SUB
    LT = q_hbm.shape[1] // SUB
    tok = q_hbm.shape[0]
    ctx = lax.axis_index("ctx")
    f = lax.axis_index("fsdp")
    x, z = ctx // Z, ctx % Z

    def dev(xx, zz):
        return (((xx + X) % X) * Z + (zz + Z) % Z, f)

    def wrap(zz):
        return (zz + Z) % Z

    barrier = pltpu.get_barrier_semaphore()
    partners = [dev(x, z + 1), dev(x, z - 1), dev(x, z + 2), dev(x, z - 2)]
    partners += [dev(x + 1, z), dev(x - 1, z), dev(x + 2, z)]
    partners += [((ctx + 1) % C, f), ((ctx + C - 1) % C, f)]
    partners += [(ctx, (f + s) % NF) for s in range(1, NF)]
    for who in partners:
        pl.semaphore_signal(barrier, inc=1, device_id=who, device_id_type=MESH)

    loads = [(k_hbm, k), (v_hbm, v), (f_hbm, filt), (q_hbm, q), (og_hbm, og)]
    loads = [pltpu.make_async_copy(a, b, load_sem.at[i]) for i, (a, b) in enumerate(loads)]
    own = pltpu.make_async_copy(w_hbm, w.at[x, pl.ds(z * rows, rows), :], own_sem)
    own.start()
    for c in loads:
        c.start()
    pl.semaphore_wait(barrier, len(partners))

    def a_ref(xx, zz):
        return w.at[(xx + X) % X, pl.ds(pl.multiple_of(wrap(zz) * rows, rows), rows), pl.ds(0, CA)]

    def b_ref(zz):
        return w.at[:, pl.ds(pl.multiple_of(wrap(zz) * rows, rows), rows), pl.ds(CA, cols - CA)]

    def remote(src, dst, ssem, rsem, who):
        pltpu.make_async_remote_copy(
            src_ref=src, dst_ref=dst, send_sem=ssem, recv_sem=rsem, device_id=who, device_id_type=MESH
        ).start()

    def wait(ref, sem):
        pltpu.make_async_copy(ref, ref, sem).wait()

    def chain_a(d, o, dist, src=None):
        sgn = 1 - 2 * d
        ref = a_ref(x, z - sgn * o)
        remote(ref if src is None else src, ref, za_send, za.at[d, o + dist], dev(x, z + sgn * dist))

    def chain_b(d, o, dist):
        sgn = 1 - 2 * d
        ref = b_ref(z - sgn * o)
        remote(ref, ref, zb_send, zb.at[d, o + dist], dev(x, z + sgn * dist))

    def spread(zs, src=None):
        ref = a_ref(x, zs)
        for side in (0, 1):
            remote(ref if src is None else src, ref, xa_send, xr.at[side, wrap(zs)], dev(x + 1 - 2 * side, z))

    def relay(zs):
        p = wrap(zs) % 2
        ref = a_ref(x - 1 + 2 * p, zs)
        wait(ref, xr.at[p, wrap(zs)])
        remote(ref, ref, xa_send, xrel.at[wrap(zs)], dev(x + 1 - 2 * p, z))

    own_a = w_hbm.at[:, pl.ds(0, CA)]
    for d in (0, 1):
        chain_a(d, 0, 2, own_a)
    for d in (0, 1):
        chain_a(d, 0, 1, own_a)
    own_b = w_hbm.at[:, pl.ds(CA, cols - CA)]
    my_b = w.at[x, pl.ds(pl.multiple_of(z * rows, rows), rows), pl.ds(CA, cols - CA)]
    for i, s in enumerate((1, 3, 2)):
        remote(own_b, my_b, xb_send, xb.at[i], dev(x + s, z))
    spread(z, own_a)

    loads[0].wait()
    loads[1].wait()
    for j in range(LT):
        lanes = slice(j * SUB, (j + 1) * SUB)
        prod = k[:, lanes].astype(F32) * v[:, lanes].astype(F32)
        ext[j, tok:, :] = prod.astype(BF)

    @pl.when(ctx < C - 1)
    def _():
        remote(ext.at[:, pl.ds(tok, tok), :], ext.at[:, pl.ds(0, tok), :], p_send, p_recv, ((ctx + 1) % C, f))

    @pl.when(ctx == 0)
    def _():
        ext[:, 0:tok, :] = jnp.zeros((LT, tok, SUB), BF)

    own.wait()
    for i in range(3):
        wait(my_b, xb.at[i])
    for d in (0, 1):
        chain_b(d, 0, 2)
    for d in (0, 1):
        chain_b(d, 0, 1)

    def step(m):
        wait(a_ref(x, z - 2 * m), za.at[0, 2 * m])

        @pl.when(m < M)
        def _():
            chain_a(0, 2 * m, 2)
            wait(a_ref(x, z + 2 * m), za.at[1, 2 * m])

            @pl.when(m < M - 1)
            def _():
                chain_a(1, 2 * m, 2)

            chain_a(0, 2 * m, 1)
            chain_a(1, 2 * m, 1)

        wait(b_ref(z - 2 * m), zb.at[0, 2 * m])

        @pl.when(m < M)
        def _():
            chain_b(0, 2 * m, 2)
            wait(b_ref(z + 2 * m), zb.at[1, 2 * m])

            @pl.when(m < M - 1)
            def _():
                chain_b(1, 2 * m, 2)

            chain_b(0, 2 * m, 1)
            chain_b(1, 2 * m, 1)
            spread(z + 2 * m)

        spread(z - 2 * m)
        for d in (0, 1):
            sgn = 1 - 2 * d
            zs = z - sgn * (2 * m - 1)
            wait(a_ref(x, zs), za.at[d, 2 * m - 1])
            spread(zs)
            wait(b_ref(zs), zb.at[d, 2 * m - 1])

        @pl.when(m > 1)
        def _():
            for zs in (z - 2 * m + 2, z + 2 * m - 2, z - 2 * m + 3, z + 2 * m - 3):
                relay(zs)

        @pl.when(m == 1)
        def _():
            relay(z)

    zg = z * rows // SUB
    per = SUB // rows

    def dgate(group):
        for i in range(per):
            zs = group * per + i
            p = zs % 2
            wait(a_ref(x + 1 - 2 * p, zs), xr.at[1 - p, zs])
            wait(a_ref(x + 2, zs), xrel.at[zs])
        at = pl.ds(pl.multiple_of(group * SUB, SUB), SUB)
        for xx in range(X):
            part = lax.dot_general(
                og[...], w[xx, at, :], (((1,), (1,)), ((), ())), preferred_element_type=F32
            ).astype(BF)
            sub = xx * NG + group
            owner, lane = sub // LT, sub % LT

            @pl.when(owner == f)
            def _():
                recv[f, lane, :, :] = part

            @pl.when(owner != f)
            def _():
                stage[sub, :, :] = part
                remote(stage.at[sub], recv.at[f, lane], r_send, r_recv.at[f, lane], (ctx, owner))

    def mixed(lo, hi):
        def body(g, carry):
            at = pl.ds(pl.multiple_of(g * SUB, SUB), SUB)
            acc = pg[...]
            for xx in range(X):
                acc = acc + jnp.dot(gated[xx * NG + g], w[xx, at, :], preferred_element_type=F32)
            pg[...] = acc
            return carry

        lax.fori_loop(lo, hi, body, 0)

    def bands():
        loads[2].wait()
        taps = filt[...].astype(BF)
        i0 = lax.broadcasted_iota(jnp.int32, (SUB, 2 * SUB), 0)
        i1 = lax.broadcasted_iota(jnp.int32, (SUB, 2 * SUB), 1)
        flip = jnp.where(i0 + i1 == SUB, 1.0, 0.0).astype(BF)
        keep = jnp.where(i0 == i1, 1.0, 0.0).astype(BF)
        pg_f = jnp.dot(taps, flip, preferred_element_type=F32)
        pg_b = jnp.dot(taps, keep, preferred_element_type=F32)
        return pg_f, pg_b

    def build(base, band):
        for g in range(base.shape[0]):
            row = jnp.broadcast_to(base[g : g + 1, :], (SUB, 2 * SUB))
            band[g * SUB : (g + 1) * SUB, :] = pltpu.roll(row, 0, 1, stride=1, stride_axis=0).astype(BF)

    lane_group = lax.broadcasted_iota(jnp.int32, (tok, SUB), 1) // 16

    def apply(band, lo, hi, data, j):
        n = SUB // 16
        res = jnp.dot(band[j * n * SUB : (j + 1) * n * SUB, lo:hi], data, preferred_element_type=F32)
        out = res[0:SUB]
        for g in range(1, n):
            out = jnp.where(lane_group == g, res[g * SUB : (g + 1) * SUB], out)
        return out

    step(1)
    base_f, base_b = bands()
    build(base_f, band_f)
    step(2)

    @pl.when(ctx > 0)
    def _():
        wait(ext.at[:, pl.ds(0, tok), :], p_recv)

    loads[3].wait()
    for j in range(LT):
        cv = apply(band_f, 0, 2 * SUB, ext[j], j)
        conv[j, :, :] = cv
        gated[f * LT + j, :, :] = (q[:, j * SUB : (j + 1) * SUB].astype(F32) * cv).astype(BF)
    mine = gated.at[pl.ds(f * LT, LT)]
    for s in range(1, NF):
        remote(mine, mine, g_send, g_recv.at[f], (ctx, (f + s) % NF))
    build(base_b, band_b)
    loads[4].wait()

    def loop(kk, carry):
        step(2 * kk + 1)

        def groups(i, c):
            dgate((zg + (1 - 2 * i) * (kk - 1) + NG) % NG)
            return c

        lax.fori_loop(0, jnp.where(kk == 1, 1, 2), groups, 0)
        step(2 * kk + 2)
        return carry

    lax.fori_loop(1, M // 2, loop, 0)
    for zs in (z - 2 * M, z - 2 * M + 1, z + 2 * M - 1):
        relay(zs)

    def last_groups(i, c):
        dgate((zg + M // 2 - 1 + i) % NG)
        return c

    lax.fori_loop(0, 2 if M == 2 else 3, last_groups, 0)

    for s in range(1, NF):
        src = (f + s) % NF
        wait(gated.at[pl.ds(src * LT, LT)], g_recv.at[src])
    pg[...] = jnp.zeros_like(pg)
    mixed(0, NG // 2)

    for j in range(LT):
        total = recv[f, j, :, :].astype(F32)
        for s in range(1, NF):
            src = (f + s) % NF
            wait(recv.at[src, j], r_recv.at[src, j])
            total = total + recv[src, j, :, :].astype(F32)
        lanes = slice(j * SUB, (j + 1) * SUB)
        cg[j, :, :] = (total * q[:, lanes].astype(F32)).astype(BF)
        qg_o[:, lanes] = (total * conv[j, :, :]).astype(BF)

        @pl.when(ctx > 0)
        def _():
            remote(cg.at[j], nxt.at[j], c_send.at[j], c_recv.at[j], ((ctx + C - 1) % C, f))

    mixed(NG // 2, NG)
    mix_o[...] = pg[...].astype(BF)
    for j in range(LT):
        conv[j, :, :] = apply(band_b, 0, SUB, cg[j], j)

    @pl.when(ctx == C - 1)
    def _():
        nxt[...] = jnp.zeros_like(nxt)

    for j in range(LT):
        @pl.when(ctx < C - 1)
        def _():
            wait(nxt.at[j], c_recv.at[j])

        lanes = slice(j * SUB, (j + 1) * SUB)
        both = conv[j, :, :] + apply(band_b, SUB, 2 * SUB, nxt[j], j)
        kg_o[:, lanes] = (both * v[:, lanes].astype(F32)).astype(BF)
        vg_o[:, lanes] = (both * k[:, lanes].astype(F32)).astype(BF)

    wait(w.at[0, pl.ds(0, (Z - 1) * rows), pl.ds(0, CA)], za_send)
    wait(w.at[pl.ds(0, 3), :, pl.ds(0, CA)], xa_send)
    wait(w.at[:, pl.ds(0, (Z - 1) * rows), pl.ds(CA, cols - CA)], zb_send)
    wait(w.at[pl.ds(0, 3), pl.ds(0, rows), pl.ds(CA, cols - CA)], xb_send)
    wait(gated.at[pl.ds(0, (NF - 1) * LT)], g_send)
    wait(gated.at[pl.ds(0, (NF - 1) * LT)], r_send)

    @pl.when(ctx < C - 1)
    def _():
        wait(ext.at[:, pl.ds(0, tok), :], p_send)

    @pl.when(ctx > 0)
    def _():
        for j in range(LT):
            wait(cg.at[j], c_send.at[j])


def solution(mesh):
    NF = mesh.shape["fsdp"]
    X = X_CHIPS
    Z = mesh.shape["ctx"] // X

    def on_device(q, k, v, f, w, og):
        tok, ch = q.shape
        lt = ch // SUB
        subs = NF * lt
        rows, cols = w.shape
        dma = pltpu.SemaphoreType.DMA
        out = jax.ShapeDtypeStruct((tok, ch), BF)
        return pl.pallas_call(
            functools.partial(kernel, X, Z, NF),
            out_shape=(jax.ShapeDtypeStruct((tok, cols), BF), out, out, out),
            in_specs=[pl.BlockSpec(memory_space=pl.ANY)] * 6,
            out_specs=tuple([pl.BlockSpec(memory_space=pltpu.VMEM)] * 4),
            scratch_shapes=[
                pltpu.VMEM((tok, ch), BF),
                pltpu.VMEM((tok, ch), BF),
                pltpu.VMEM((tok, ch), BF),
                pltpu.VMEM((tok, cols), BF),
                pltpu.VMEM(f.shape, F32),
                pltpu.VMEM((X, Z * rows, cols), BF),
                pltpu.VMEM((lt, 2 * tok, SUB), BF),
                pltpu.VMEM((f.shape[0] * SUB, 2 * SUB), BF),
                pltpu.VMEM((f.shape[0] * SUB, 2 * SUB), BF),
                pltpu.VMEM((lt, tok, SUB), F32),
                pltpu.VMEM((subs, tok, SUB), BF),
                pltpu.VMEM((subs, tok, SUB), BF),
                pltpu.VMEM((NF, lt, tok, SUB), BF),
                pltpu.VMEM((lt, tok, SUB), BF),
                pltpu.VMEM((lt, tok, SUB), BF),
                pltpu.VMEM((tok, cols), F32),
                dma((5,)), dma, dma, dma, dma, dma,
                dma((2, Z // 2 + 1)), dma((2, Z)), dma((Z,)), dma((2, Z // 2 + 1)), dma((3,)),
                dma, dma((NF,)), dma, dma((NF, lt)), dma, dma, dma((lt,)), dma((lt,)),
            ],
            compiler_params=pltpu.CompilerParams(
                collective_id=0, has_side_effects=True, vmem_limit_bytes=48 * 1024 * 1024
            ),
        )(q, k, v, f, w, og)

    wide = P("ctx", "fsdp")
    return jax.shard_map(
        on_device,
        mesh=mesh,
        in_specs=(wide, wide, wide, P("fsdp", None), wide, wide),
        out_specs=(wide, wide, wide, wide),
        check_vma=False,
    )
```

```python
import functools

import jax
import jax.numpy as jnp
from jax import lax
from jax.experimental import pallas as pl
from jax.experimental.pallas import tpu as pltpu
from jax.sharding import PartitionSpec as P

MESH = pl.DeviceIdType.MESH
BF = jnp.bfloat16
F32 = jnp.float32
SUB = 128
X_CHIPS = 4
STRIDE = 4


def broadcast_tree(size, stride):
    parent = {}
    for sgn in (1, -1):
        top = size // 2 if sgn == 1 else size // 2 - 1
        for o in range(1, top + 1):
            r = o % stride
            up = o - r + stride
            if r == 0:
                p = o - stride
            elif 2 * r > stride and up <= top:
                p = up
            else:
                p = o - r
            parent[sgn * o] = sgn * p
    kids = {}
    for o, p in parent.items():
        kids.setdefault(p, []).append(o)
    for p in kids:
        kids[p].sort(key=lambda o: -abs(o - p))
    return kids


def kernel(
    X, Z, NF,
    q_hbm, k_hbm, v_hbm, f_hbm, w_hbm, og_hbm,
    mix_o, qg_o, pg_o,
    q, k, v, filt, w, og, ext, band_f, band_b, conv, g_own, gated, stage, recv, cg, nxt, mstage, mrecv,
    load_sem, w_send, w_recv, og_send, og_recv, og_own, g_send, g_recv, g_self, r_send, r_recv,
    p_send, p_recv, c_send, c_recv, m_send, m_recv,
):
    C = X * Z
    rows, cols = w_hbm.shape
    tok, chans = q_hbm.shape
    LT = chans // SUB
    line = Z * rows
    HP = line // chans
    NG = line // SUB
    per = SUB // rows
    ctx = lax.axis_index("ctx")
    f = lax.axis_index("fsdp")
    x, z = ctx // Z, ctx % Z
    kids = broadcast_tree(Z, STRIDE)

    def dev(xx, zz, ff=None):
        return (((xx + X) % X) * Z + (zz + Z) % Z, f if ff is None else ff)

    home = f // HP == x
    barrier = pltpu.get_barrier_semaphore()
    jumps = sorted({o - p for p in kids for o in kids[p]} | {p - o for p in kids for o in kids[p]})
    partners = [dev(x, z + o) for o in jumps]
    partners += [dev(x + 1, z), dev(x - 1, z), dev(x + 2, z)]
    partners += [((ctx + 1) % C, f), ((ctx + C - 1) % C, f)]

    def hello(who):
        pl.semaphore_signal(barrier, inc=1, device_id=who, device_id_type=MESH)

    for who in partners:
        hello(who)
    for xx in range(X):
        for h in range(HP):
            ff = HP * x + h

            @pl.when(jnp.logical_or(xx != x, ff != f))
            def _():
                hello(dev(xx, z, ff))

    for ff in range(NF):
        @pl.when(jnp.logical_or(jnp.logical_not(home), ff != f))
        def _():
            hello(dev(f // HP, z, ff))

    loads = [(k_hbm, k), (v_hbm, v), (f_hbm, filt), (q_hbm, q)]
    loads = [pltpu.make_async_copy(a, b, load_sem.at[i]) for i, (a, b) in enumerate(loads)]
    mine_w = w.at[pl.ds(pl.multiple_of(z * rows, rows), rows), :]
    own_w = pltpu.make_async_copy(w_hbm, mine_w, w_recv.at[0])
    mine_og = og.at[pl.ds(pl.multiple_of(x * tok, tok), tok), :]
    own_og = pltpu.make_async_copy(og_hbm, mine_og, og_own)
    own_w.start()
    for c in loads:
        c.start()
    own_og.start()
    extra = X * HP + NF
    pl.semaphore_wait(barrier, len(partners) + jnp.where(home, extra - 2, extra))

    def remote(src, dst, ssem, rsem, who):
        pltpu.make_async_remote_copy(
            src_ref=src, dst_ref=dst, send_sem=ssem, recv_sem=rsem, device_id=who, device_id_type=MESH
        ).start()

    def wait(ref, sem):
        pltpu.make_async_copy(ref, ref, sem).wait()

    def block(zs):
        return w.at[pl.ds(pl.multiple_of((zs + Z) % Z * rows, rows), rows), :]

    def pass_on(o):
        ref = block(z - o)
        if o != 0:
            wait(ref, w_recv.at[o % Z])
        for c in kids.get(o, ()):
            remote(w_hbm if o == 0 else ref, ref, w_send, w_recv.at[c % Z], dev(x, z + c - o))

    pass_on(0)
    for s in (1, 3, 2):
        remote(og_hbm, mine_og, og_send, og_recv.at[x], dev(x + s, z))

    loads[0].wait()
    loads[1].wait()
    for j in range(LT):
        lanes = slice(j * SUB, (j + 1) * SUB)
        ext[j, tok:, :] = (k[:, lanes].astype(F32) * v[:, lanes].astype(F32)).astype(BF)

    @pl.when(ctx < C - 1)
    def _():
        remote(ext.at[:, pl.ds(tok, tok), :], ext.at[:, pl.ds(0, tok), :], p_send, p_recv, ((ctx + 1) % C, f))

    @pl.when(ctx == 0)
    def _():
        ext[:, 0:tok, :] = jnp.zeros((LT, tok, SUB), BF)

    loads[2].wait()
    taps = filt[...].astype(BF)
    i0 = lax.broadcasted_iota(jnp.int32, (SUB, 2 * SUB), 0)
    i1 = lax.broadcasted_iota(jnp.int32, (SUB, 2 * SUB), 1)

    def build(picks, band):
        base = jnp.dot(taps, jnp.where(picks, 1.0, 0.0).astype(BF), preferred_element_type=F32)
        for g in range(base.shape[0]):
            row = jnp.broadcast_to(base[g : g + 1, :], (SUB, 2 * SUB))
            band[g * SUB : (g + 1) * SUB, :] = pltpu.roll(row, 0, 1, stride=1, stride_axis=0).astype(BF)

    lane_group = lax.broadcasted_iota(jnp.int32, (tok, SUB), 1) // 16

    def apply(band, lo, hi, data, j):
        n = SUB // 16
        res = jnp.dot(band[j * n * SUB : (j + 1) * n * SUB, lo:hi], data, preferred_element_type=F32)
        out = res[0:SUB]
        for g in range(1, n):
            out = jnp.where(lane_group == g, res[g * SUB : (g + 1) * SUB], out)
        return out

    zg = z // per

    def dgate(group):
        group = (group + NG) % NG
        for i in range(per):
            zs = group * per + i
            o = (z - zs + Z) % Z

            @pl.when(o % STRIDE != 0)
            def _():
                wait(block(zs), w_recv.at[o])

        at = pl.ds(pl.multiple_of(group * SUB, SUB), SUB)
        part = lax.dot_general(
            og[...], w[at, :], (((1,), (1,)), ((), ())), preferred_element_type=F32
        ).astype(BF)
        base = x * line + group * SUB
        owner, lane = base // chans, base % chans // SUB
        for xx in range(X):
            mine = jnp.logical_and(xx == x, owner == f)
            piece = part[xx * tok : (xx + 1) * tok, :]

            @pl.when(mine)
            def _():
                recv[f, lane, :, :] = piece

            @pl.when(jnp.logical_not(mine))
            def _():
                stage[group, xx, :, :] = piece
                remote(stage.at[group, xx], recv.at[f, lane], r_send, r_recv.at[f, lane], dev(xx, z, owner))

    def dgates(first, count, step=1):
        def body(i, c):
            dgate(zg + first + i * step)
            return c

        lax.fori_loop(0, count, body, 0)

    build(i0 + i1 == SUB, band_f)
    last = Z // 2 // STRIDE
    pass_on(STRIDE)
    if last > 1:
        pass_on(-STRIDE)

    @pl.when(ctx > 0)
    def _():
        wait(ext.at[:, pl.ds(0, tok), :], p_recv)

    loads[3].wait()
    for j in range(LT):
        lanes = slice(j * SUB, (j + 1) * SUB)
        cv = apply(band_f, 0, 2 * SUB, ext[j], j)
        conv[j, :, :] = cv
        g_own[:, lanes] = (q[:, lanes].astype(F32) * cv).astype(BF)

    def gated_slot(xx, h):
        return gated.at[pl.ds(pl.multiple_of(xx * tok, tok), tok), pl.ds(pl.multiple_of(h * chans, chans), chans)]

    for s in range(NF):
        ff = (f + s) % NF

        def send_gated():
            remote(g_own, gated_slot(x, f % HP), g_send, g_recv.at[x, f % HP], dev(f // HP, z, ff))

        if s == 0:
            pl.when(jnp.logical_not(home))(send_gated)
        else:
            send_gated()

    @pl.when(home)
    def _():
        pltpu.make_async_copy(g_own, gated_slot(x, f % HP), g_self).start()

    if last > 1:
        pass_on(2 * STRIDE)
        if last > 2:
            pass_on(-2 * STRIDE)
    build(i0 == i1, band_b)
    own_w.wait()
    own_og.wait()
    for s in range(1, X):
        src = (x + s) % X
        wait(og.at[pl.ds(pl.multiple_of(src * tok, tok), tok), :], og_recv.at[src])
    done = 0
    if last > 1:
        dgates(0, 1)
        done = 1
    for m in range(3, last + 1):
        pass_on(m * STRIDE)
        if m < last:
            pass_on(-m * STRIDE)
        dgates(m - 2, 2, -2 * (m - 2))
        done += 2
    dgates(done // 2 + 1 if done else 0, NG - done)

    for xx in range(X):
        for h in range(HP):
            @pl.when(jnp.logical_or(xx != x, HP * x + h != f))
            def _():
                wait(gated_slot(xx, h), g_recv.at[xx, h])

    @pl.when(home)
    def _():
        wait(g_own, g_self)

    for s in (2, 1, 3, 0):
        xx = (x + s) % X
        part = jnp.dot(
            gated[pl.ds(pl.multiple_of(xx * tok, tok), tok), :], w[...], preferred_element_type=F32
        )
        if s == 0:
            mix_o[...] = part
        else:
            mstage[s, :, :] = part.astype(BF)
            remote(mstage.at[s], mrecv.at[x], m_send, m_recv.at[x], dev(xx, z))

    for j in range(LT):
        total = jnp.zeros((tok, SUB), F32)
        for s in range(NF):
            src = (f + s) % NF
            if s == 0:
                @pl.when(jnp.logical_not(home))
                def _():
                    wait(recv.at[src, j], r_recv.at[src, j])
            else:
                wait(recv.at[src, j], r_recv.at[src, j])
            total = total + recv[src, j, :, :].astype(F32)
        lanes = slice(j * SUB, (j + 1) * SUB)
        cg[j, :, :] = (total * q[:, lanes].astype(F32)).astype(BF)
        qg_o[:, lanes] = total * conv[j, :, :]

        @pl.when(ctx > 0)
        def _():
            remote(cg.at[j], nxt.at[j], c_send.at[j], c_recv.at[j], ((ctx + C - 1) % C, f))

    for j in range(LT):
        conv[j, :, :] = apply(band_b, 0, SUB, cg[j], j)

    mix = mix_o[...]
    for s in range(1, X):
        src = (x + s) % X
        wait(mrecv.at[src], m_recv.at[src])
        mix = mix + mrecv[src, :, :].astype(F32)
    mix_o[...] = mix

    @pl.when(ctx == C - 1)
    def _():
        nxt[...] = jnp.zeros_like(nxt)

    for j in range(LT):
        @pl.when(ctx < C - 1)
        def _():
            wait(nxt.at[j], c_recv.at[j])

        pg_o[:, j * SUB : (j + 1) * SUB] = conv[j, :, :] + apply(band_b, SUB, 2 * SUB, nxt[j], j)

    wait(w.at[pl.ds(0, (Z - 1) * rows), :], w_send)
    wait(og.at[pl.ds(0, (X - 1) * tok), :], og_send)
    wait(mrecv.at[pl.ds(0, X - 1)], m_send)
    for sem in (g_send, r_send):
        @pl.when(home)
        def _():
            wait(recv.at[pl.ds(0, NF - 1)], sem)

        @pl.when(jnp.logical_not(home))
        def _():
            wait(recv, sem)

    @pl.when(ctx < C - 1)
    def _():
        wait(ext.at[:, pl.ds(0, tok), :], p_send)

    @pl.when(ctx > 0)
    def _():
        for j in range(LT):
            wait(cg.at[j], c_send.at[j])


def solution(mesh):
    NF = mesh.shape["fsdp"]
    X = X_CHIPS
    Z = mesh.shape["ctx"] // X

    def on_device(q, k, v, f, w, og):
        tok, ch = q.shape
        lt = ch // SUB
        rows, cols = w.shape
        line = Z * rows
        dma = pltpu.SemaphoreType.DMA
        mix, qg, pg = pl.pallas_call(
            functools.partial(kernel, X, Z, NF),
            out_shape=(
                jax.ShapeDtypeStruct((tok, cols), F32),
                jax.ShapeDtypeStruct((tok, ch), F32),
                jax.ShapeDtypeStruct((tok, ch), F32),
            ),
            in_specs=[pl.BlockSpec(memory_space=pltpu.HBM)] * 6,
            out_specs=tuple([pl.BlockSpec(memory_space=pltpu.VMEM)] * 3),
            scratch_shapes=[
                pltpu.VMEM((tok, ch), BF),
                pltpu.VMEM((tok, ch), BF),
                pltpu.VMEM((tok, ch), BF),
                pltpu.VMEM(f.shape, F32),
                pltpu.VMEM((line, cols), BF),
                pltpu.VMEM((X * tok, cols), BF),
                pltpu.VMEM((lt, 2 * tok, SUB), BF),
                pltpu.VMEM((f.shape[0] * SUB, 2 * SUB), BF),
                pltpu.VMEM((f.shape[0] * SUB, 2 * SUB), BF),
                pltpu.VMEM((lt, tok, SUB), F32),
                pltpu.VMEM((tok, ch), BF),
                pltpu.VMEM((X * tok, line), BF),
                pltpu.VMEM((line // SUB, X, tok, SUB), BF),
                pltpu.VMEM((NF, lt, tok, SUB), BF),
                pltpu.VMEM((lt, tok, SUB), BF),
                pltpu.VMEM((lt, tok, SUB), BF),
                pltpu.VMEM((X, tok, cols), BF),
                pltpu.VMEM((X, tok, cols), BF),
                dma((4,)), dma, dma((Z,)), dma, dma((X,)), dma, dma, dma((X, line // ch)), dma,
                dma, dma((NF, lt)), dma, dma, dma((lt,)), dma((lt,)), dma, dma((X,)),
            ],
            compiler_params=pltpu.CompilerParams(
                collective_id=0, has_side_effects=True, vmem_limit_bytes=40 * 1024 * 1024
            ),
        )(*[pltpu.with_memory_space_constraint(a, pltpu.HBM) for a in (q, k, v, f, w, og)])
        kg = (pg * v.astype(F32)).astype(BF)
        vg = (pg * k.astype(F32)).astype(BF)
        return mix.astype(BF), qg.astype(BF), kg, vg

    wide = P("ctx", "fsdp")
    return jax.shard_map(
        on_device,
        mesh=mesh,
        in_specs=(wide, wide, wide, P("fsdp", None), wide, wide),
        out_specs=(wide, wide, wide, wide),
        check_vma=False,
    )
```

```python
import functools

import jax
import jax.numpy as jnp
from jax import lax
from jax.experimental import pallas as pl
from jax.experimental.pallas import tpu as pltpu
from jax.sharding import PartitionSpec as P

MESH = pl.DeviceIdType.MESH
BF = jnp.bfloat16
F32 = jnp.float32
SUB = 128
X_CHIPS = 4
STRIDE = 4


def broadcast_tree(size, stride):
    parent = {}
    for sgn in (1, -1):
        top = size // 2 if sgn == 1 else size // 2 - 1
        for o in range(1, top + 1):
            r = o % stride
            up = o - r + stride
            if r == 0:
                p = o - stride
            elif 2 * r > stride and up <= top:
                p = up
            else:
                p = o - r
            parent[sgn * o] = sgn * p
    kids = {}
    for o, p in parent.items():
        kids.setdefault(p, []).append(o)
    for p in kids:
        kids[p].sort(key=lambda o: -abs(o - p))
    return kids


def kernel(
    X, Z, NF,
    q_hbm, k_hbm, v_hbm, f_hbm, w_hbm, og_hbm,
    mix_o, qg_o, pg_o,
    q, k, v, filt, w, og, ext, band_f, band_b, conv, g_own, gated, gpass, stage, recv, cg, nxt, mstage, mrecv,
    load_sem, w_send, w_recv, og_send, og_recv, og_own, g_send, gp_recv, gx_recv, gt_send, gt_recv, g_self, r_send, r_recv,
    p_send, p_recv, c_send, c_recv, m_send, m_recv,
):
    C = X * Z
    rows, cols = w_hbm.shape
    tok, chans = q_hbm.shape
    LT = chans // SUB
    line = Z * rows
    HP = line // chans
    NG = line // SUB
    per = SUB // rows
    ctx = lax.axis_index("ctx")
    f = lax.axis_index("fsdp")
    x, z = ctx // Z, ctx % Z
    kids = broadcast_tree(Z, STRIDE)

    def dev(xx, zz, ff=None):
        return (((xx + X) % X) * Z + (zz + Z) % Z, f if ff is None else ff)

    y, core = f // HP, f % HP
    twin = HP * y + (core + 1) % HP
    home = y == x
    barrier = pltpu.get_barrier_semaphore()
    jumps = sorted({o - p for p in kids for o in kids[p]} | {p - o for p in kids for o in kids[p]})
    partners = [dev(x, z + o) for o in jumps]
    partners += [dev(x + 1, z), dev(x - 1, z), dev(x + 2, z)]
    partners += [((ctx + 1) % C, f), ((ctx + C - 1) % C, f)]
    partners += [dev(x, z, (f + HP * t) % NF) for t in range(1, X)] + [dev(x, z, twin)]

    def hello(who):
        pl.semaphore_signal(barrier, inc=1, device_id=who, device_id_type=MESH)

    for who in partners:
        hello(who)
    for xx in range(X):
        for h in range(HP):
            ff = HP * x + h

            @pl.when(jnp.logical_or(xx != x, ff != f))
            def _():
                hello(dev(xx, z, ff))

    for ff in range(NF):
        @pl.when(jnp.logical_or(jnp.logical_not(home), ff != f))
        def _():
            hello(dev(f // HP, z, ff))

    loads = [(k_hbm, k), (v_hbm, v), (f_hbm, filt), (q_hbm, q)]
    loads = [pltpu.make_async_copy(a, b, load_sem.at[i]) for i, (a, b) in enumerate(loads)]
    mine_w = w.at[pl.ds(pl.multiple_of(z * rows, rows), rows), :]
    own_w = pltpu.make_async_copy(w_hbm, mine_w, w_recv.at[0])
    mine_og = og.at[pl.ds(pl.multiple_of(x * tok, tok), tok), :]
    own_og = pltpu.make_async_copy(og_hbm, mine_og, og_own)
    own_w.start()
    for c in loads:
        c.start()
    own_og.start()
    extra = X * HP + NF
    pl.semaphore_wait(barrier, len(partners) + jnp.where(home, extra - 2, extra))

    def remote(src, dst, ssem, rsem, who):
        pltpu.make_async_remote_copy(
            src_ref=src, dst_ref=dst, send_sem=ssem, recv_sem=rsem, device_id=who, device_id_type=MESH
        ).start()

    def wait(ref, sem):
        pltpu.make_async_copy(ref, ref, sem).wait()

    def block(zs):
        return w.at[pl.ds(pl.multiple_of((zs + Z) % Z * rows, rows), rows), :]

    def pass_on(o):
        ref = block(z - o)
        if o != 0:
            wait(ref, w_recv.at[o % Z])
        for c in kids.get(o, ()):
            remote(w_hbm if o == 0 else ref, ref, w_send, w_recv.at[c % Z], dev(x, z + c - o))

    pass_on(0)
    for s in (1, 3, 2):
        remote(og_hbm, mine_og, og_send, og_recv.at[x], dev(x + s, z))

    loads[0].wait()
    loads[1].wait()
    for j in range(LT):
        lanes = slice(j * SUB, (j + 1) * SUB)
        ext[j, tok:, :] = (k[:, lanes].astype(F32) * v[:, lanes].astype(F32)).astype(BF)

    @pl.when(ctx < C - 1)
    def _():
        remote(ext.at[:, pl.ds(tok, tok), :], ext.at[:, pl.ds(0, tok), :], p_send, p_recv, ((ctx + 1) % C, f))

    @pl.when(ctx == 0)
    def _():
        ext[:, 0:tok, :] = jnp.zeros((LT, tok, SUB), BF)

    loads[2].wait()
    taps = filt[...].astype(BF)
    i0 = lax.broadcasted_iota(jnp.int32, (SUB, 2 * SUB), 0)
    i1 = lax.broadcasted_iota(jnp.int32, (SUB, 2 * SUB), 1)

    def build(picks, band):
        base = jnp.dot(taps, jnp.where(picks, 1.0, 0.0).astype(BF), preferred_element_type=F32)
        for g in range(base.shape[0]):
            row = jnp.broadcast_to(base[g : g + 1, :], (SUB, 2 * SUB))
            band[g * SUB : (g + 1) * SUB, :] = pltpu.roll(row, 0, 1, stride=1, stride_axis=0).astype(BF)

    lane_group = lax.broadcasted_iota(jnp.int32, (tok, SUB), 1) // 16

    def apply(band, lo, hi, data, j):
        n = SUB // 16
        res = jnp.dot(band[j * n * SUB : (j + 1) * n * SUB, lo:hi], data, preferred_element_type=F32)
        out = res[0:SUB]
        for g in range(1, n):
            out = jnp.where(lane_group == g, res[g * SUB : (g + 1) * SUB], out)
        return out

    zg = z // per

    def dgate(group):
        group = (group + NG) % NG
        for i in range(per):
            zs = group * per + i
            o = (z - zs + Z) % Z

            @pl.when(o % STRIDE != 0)
            def _():
                wait(block(zs), w_recv.at[o])

        at = pl.ds(pl.multiple_of(group * SUB, SUB), SUB)
        part = lax.dot_general(
            og[...], w[at, :], (((1,), (1,)), ((), ())), preferred_element_type=F32
        ).astype(BF)
        base = x * line + group * SUB
        owner, lane = base // chans, base % chans // SUB
        for xx in range(X):
            mine = jnp.logical_and(xx == x, owner == f)
            piece = part[xx * tok : (xx + 1) * tok, :]

            @pl.when(mine)
            def _():
                recv[f, lane, :, :] = piece

            @pl.when(jnp.logical_not(mine))
            def _():
                stage[group, xx, :, :] = piece
                remote(stage.at[group, xx], recv.at[f, lane], r_send, r_recv.at[f, lane], dev(xx, z, owner))

    def dgates(first, count, step=1):
        def body(i, c):
            dgate(zg + first + i * step)
            return c

        lax.fori_loop(0, count, body, 0)

    build(i0 + i1 == SUB, band_f)
    last = Z // 2 // STRIDE
    pass_on(STRIDE)
    if last > 1:
        pass_on(-STRIDE)

    @pl.when(ctx > 0)
    def _():
        wait(ext.at[:, pl.ds(0, tok), :], p_recv)

    loads[3].wait()
    for j in range(LT):
        lanes = slice(j * SUB, (j + 1) * SUB)
        cv = apply(band_f, 0, 2 * SUB, ext[j], j)
        conv[j, :, :] = cv
        g_own[:, lanes] = (q[:, lanes].astype(F32) * cv).astype(BF)

    def gated_slot(xx, h):
        return gated.at[pl.ds(pl.multiple_of(xx * tok, tok), tok), pl.ds(pl.multiple_of(h * chans, chans), chans)]

    for t in (2, 1, 3):
        who = dev(x, z, (f + HP * t) % NF)

        @pl.when(home)
        def _():
            remote(g_own, gated_slot(x, core), g_send, gp_recv.at[y], who)

        @pl.when(jnp.logical_not(home))
        def _():
            remote(g_own, gpass.at[y], g_send, gp_recv.at[y], who)

    @pl.when(home)
    def _():
        pltpu.make_async_copy(g_own, gated_slot(x, core), g_self).start()

    @pl.when(jnp.logical_not(home))
    def _():
        remote(g_own, gated_slot(x, core), g_send, gx_recv.at[x], dev(y, z))

    def along_x():
        for t in (2, 1, 3):
            y0 = (x + t) % X

            @pl.when(y0 != y)
            def _():
                wait(gpass.at[y0], gp_recv.at[y0])
                remote(gpass.at[y0], gated_slot(x, core), g_send, gx_recv.at[x], dev(y0, z))

    def to_twin():
        for t in range(X):
            x0 = (x + t) % X
            ref = gated_slot(x0, core)
            if t == 0:
                @pl.when(home)
                def _():
                    wait(ref, g_self)

                @pl.when(jnp.logical_not(home))
                def _():
                    wait(ref, gp_recv.at[x])
            else:
                wait(ref, gx_recv.at[x0])
            remote(ref, ref, gt_send, gt_recv.at[x0], dev(x, z, twin))

    if last > 1:
        pass_on(2 * STRIDE)
        if last > 2:
            pass_on(-2 * STRIDE)
    build(i0 == i1, band_b)
    along_x()
    own_w.wait()
    own_og.wait()
    for s in range(1, X):
        src = (x + s) % X
        wait(og.at[pl.ds(pl.multiple_of(src * tok, tok), tok), :], og_recv.at[src])
    done = 0
    if last > 1:
        dgates(0, 1)
        done = 1
    if last == 1:
        to_twin()
    for m in range(3, last + 1):
        pass_on(m * STRIDE)
        if m < last:
            pass_on(-m * STRIDE)
        dgates(m - 2, 2, -2 * (m - 2))
        if m == 3:
            to_twin()
        done += 2
    dgates(done // 2 + 1 if done else 0, NG - done)

    for xx in range(X):
        wait(gated_slot(xx, (core + 1) % HP), gt_recv.at[xx])

    for s in (2, 1, 3, 0):
        xx = (x + s) % X
        part = jnp.dot(
            gated[pl.ds(pl.multiple_of(xx * tok, tok), tok), :], w[...], preferred_element_type=F32
        )
        if s == 0:
            mix_o[...] = part
        else:
            mstage[s, :, :] = part.astype(BF)
            remote(mstage.at[s], mrecv.at[x], m_send, m_recv.at[x], dev(xx, z))

    for j in range(LT):
        total = jnp.zeros((tok, SUB), F32)
        for s in range(NF):
            src = (f + s) % NF
            if s == 0:
                @pl.when(jnp.logical_not(home))
                def _():
                    wait(recv.at[src, j], r_recv.at[src, j])
            else:
                wait(recv.at[src, j], r_recv.at[src, j])
            total = total + recv[src, j, :, :].astype(F32)
        lanes = slice(j * SUB, (j + 1) * SUB)
        cg[j, :, :] = (total * q[:, lanes].astype(F32)).astype(BF)
        qg_o[:, lanes] = total * conv[j, :, :]

        @pl.when(ctx > 0)
        def _():
            remote(cg.at[j], nxt.at[j], c_send.at[j], c_recv.at[j], ((ctx + C - 1) % C, f))

    for j in range(LT):
        conv[j, :, :] = apply(band_b, 0, SUB, cg[j], j)

    mix = mix_o[...]
    for s in range(1, X):
        src = (x + s) % X
        wait(mrecv.at[src], m_recv.at[src])
        mix = mix + mrecv[src, :, :].astype(F32)
    mix_o[...] = mix

    @pl.when(ctx == C - 1)
    def _():
        nxt[...] = jnp.zeros_like(nxt)

    for j in range(LT):
        @pl.when(ctx < C - 1)
        def _():
            wait(nxt.at[j], c_recv.at[j])

        pg_o[:, j * SUB : (j + 1) * SUB] = conv[j, :, :] + apply(band_b, SUB, 2 * SUB, nxt[j], j)

    wait(w.at[pl.ds(0, (Z - 1) * rows), :], w_send)
    wait(og.at[pl.ds(0, (X - 1) * tok), :], og_send)
    wait(mrecv.at[pl.ds(0, X - 1)], m_send)
    wait(gpass, gt_send)

    wait(recv.at[pl.ds(0, 2 * (X - 1))], g_send)

    @pl.when(home)
    def _():
        wait(recv.at[pl.ds(0, NF - 1)], r_send)

    @pl.when(jnp.logical_not(home))
    def _():
        wait(recv, r_send)

    @pl.when(ctx < C - 1)
    def _():
        wait(ext.at[:, pl.ds(0, tok), :], p_send)

    @pl.when(ctx > 0)
    def _():
        for j in range(LT):
            wait(cg.at[j], c_send.at[j])


def solution(mesh):
    NF = mesh.shape["fsdp"]
    X = X_CHIPS
    Z = mesh.shape["ctx"] // X

    def on_device(q, k, v, f, w, og):
        tok, ch = q.shape
        lt = ch // SUB
        rows, cols = w.shape
        line = Z * rows
        dma = pltpu.SemaphoreType.DMA
        mix, qg, pg = pl.pallas_call(
            functools.partial(kernel, X, Z, NF),
            out_shape=(
                jax.ShapeDtypeStruct((tok, cols), F32),
                jax.ShapeDtypeStruct((tok, ch), F32),
                jax.ShapeDtypeStruct((tok, ch), F32),
            ),
            in_specs=[pl.BlockSpec(memory_space=pltpu.HBM)] * 6,
            out_specs=tuple([pl.BlockSpec(memory_space=pltpu.VMEM)] * 3),
            scratch_shapes=[
                pltpu.VMEM((tok, ch), BF),
                pltpu.VMEM((tok, ch), BF),
                pltpu.VMEM((tok, ch), BF),
                pltpu.VMEM(f.shape, F32),
                pltpu.VMEM((line, cols), BF),
                pltpu.VMEM((X * tok, cols), BF),
                pltpu.VMEM((lt, 2 * tok, SUB), BF),
                pltpu.VMEM((f.shape[0] * SUB, 2 * SUB), BF),
                pltpu.VMEM((f.shape[0] * SUB, 2 * SUB), BF),
                pltpu.VMEM((lt, tok, SUB), F32),
                pltpu.VMEM((tok, ch), BF),
                pltpu.VMEM((X * tok, line), BF),
                pltpu.VMEM((X, tok, ch), BF),
                pltpu.VMEM((line // SUB, X, tok, SUB), BF),
                pltpu.VMEM((NF, lt, tok, SUB), BF),
                pltpu.VMEM((lt, tok, SUB), BF),
                pltpu.VMEM((lt, tok, SUB), BF),
                pltpu.VMEM((X, tok, cols), BF),
                pltpu.VMEM((X, tok, cols), BF),
                dma((4,)), dma, dma((Z,)), dma, dma((X,)), dma, dma, dma((X,)), dma((X,)), dma, dma((X,)), dma,
                dma, dma((NF, lt)), dma, dma, dma((lt,)), dma((lt,)), dma, dma((X,)),
            ],
            compiler_params=pltpu.CompilerParams(
                collective_id=0, has_side_effects=True, vmem_limit_bytes=40 * 1024 * 1024
            ),
        )(*[pltpu.with_memory_space_constraint(a, pltpu.HBM) for a in (q, k, v, f, w, og)])
        kg = (pg * v.astype(F32)).astype(BF)
        vg = (pg * k.astype(F32)).astype(BF)
        return mix.astype(BF), qg.astype(BF), kg, vg

    wide = P("ctx", "fsdp")
    return jax.shard_map(
        on_device,
        mesh=mesh,
        in_specs=(wide, wide, wide, P("fsdp", None), wide, wide),
        out_specs=(wide, wide, wide, wide),
        check_vma=False,
    )
```

```python
import functools

import jax
import jax.numpy as jnp
from jax import lax
from jax.experimental import pallas as pl
from jax.experimental.pallas import tpu as pltpu
from jax.sharding import PartitionSpec as P

MESH = pl.DeviceIdType.MESH
BF = jnp.bfloat16
F32 = jnp.float32
SUB = 128
X_CHIPS = 4
STRIDE = 4
CONV_AT, OG_AT, X_AT = 1, 2, 2


def broadcast_tree(size, stride):
    parent = {}
    for sgn in (1, -1):
        top = size // 2 if sgn == 1 else size // 2 - 1
        for o in range(1, top + 1):
            r = o % stride
            up = o - r + stride
            if r == 0:
                p = o - stride
            elif 2 * r > stride and up <= top:
                p = up
            elif r == 2 and stride == 4:
                p = o - 1
            else:
                p = o - r
            parent[sgn * o] = sgn * p
    kids = {}
    for o, p in parent.items():
        kids.setdefault(p, []).append(o)
    for p in kids:
        kids[p].sort(key=lambda o: -abs(o - p))
    return kids


def kernel(
    X, Z, NF,
    q_hbm, k_hbm, v_hbm, f_hbm, w_hbm, og_hbm,
    mix_o, qg_o, kg_o, vg_o,
    q, k, v, filt, w, og, ext, band_f, band_b, conv, g_own, gated, gpass, mix_f, stage, recv, cg, nxt, mstage, mrecv,
    load_sem, w_send, w_recv, og_send, og_recv, og_own, g_send, gp_recv, gx_recv, gt_send, gt_recv, g_self, r_send, r_recv,
    p_send, p_recv, c_send, c_recv, m_send, m_recv,
):
    C = X * Z
    rows, cols = w_hbm.shape
    tok, chans = q_hbm.shape
    LT = chans // SUB
    line = Z * rows
    HP = line // chans
    NG = line // SUB
    per = SUB // rows
    ctx = lax.axis_index("ctx")
    f = lax.axis_index("fsdp")
    x, z = ctx // Z, ctx % Z
    kids = broadcast_tree(Z, STRIDE)
    lead = sorted((o for o in kids if o), key=lambda o: (abs(o), -o))
    parent = {c: p for p in kids for c in kids[p]}

    def dev(xx, zz, ff=None):
        return (((xx + X) % X) * Z + (zz + Z) % Z, f if ff is None else ff)

    y, core = f // HP, f % HP
    twin = HP * y + (core + 1) % HP
    home = y == x
    barrier = pltpu.get_barrier_semaphore()
    jumps = sorted({o - p for p in kids for o in kids[p]} | {p - o for p in kids for o in kids[p]})
    partners = [dev(x, z + o) for o in jumps]
    partners += [dev(x + 1, z), dev(x - 1, z), dev(x + 2, z)]
    partners += [((ctx + 1) % C, f), ((ctx + C - 1) % C, f)]
    partners += [dev(x, z, (f + HP * t) % NF) for t in range(1, X)] + [dev(x, z, twin)]

    def hello(who):
        pl.semaphore_signal(barrier, inc=1, device_id=who, device_id_type=MESH)

    for who in partners:
        hello(who)
    for xx in range(X):
        for h in range(HP):
            ff = HP * x + h

            @pl.when(jnp.logical_or(xx != x, ff != f))
            def _():
                hello(dev(xx, z, ff))

    for ff in range(NF):
        @pl.when(jnp.logical_or(jnp.logical_not(home), ff != f))
        def _():
            hello(dev(f // HP, z, ff))

    loads = [(k_hbm, k), (v_hbm, v), (f_hbm, filt), (q_hbm, q)]
    loads = [pltpu.make_async_copy(a, b, load_sem.at[i]) for i, (a, b) in enumerate(loads)]
    mine_w = w.at[pl.ds(pl.multiple_of(z * rows, rows), rows), :]
    own_w = pltpu.make_async_copy(w_hbm, mine_w, w_recv.at[0])
    mine_og = og.at[pl.ds(pl.multiple_of(x * tok, tok), tok), :]
    own_og = pltpu.make_async_copy(og_hbm, mine_og, og_own)
    own_w.start()
    for c in loads:
        c.start()
    own_og.start()
    extra = X * HP + NF
    pl.semaphore_wait(barrier, len(partners) + jnp.where(home, extra - 2, extra))

    def remote(src, dst, ssem, rsem, who):
        pltpu.make_async_remote_copy(
            src_ref=src, dst_ref=dst, send_sem=ssem, recv_sem=rsem, device_id=who, device_id_type=MESH
        ).start()

    def wait(ref, sem):
        pltpu.make_async_copy(ref, ref, sem).wait()

    def block(zs):
        return w.at[pl.ds(pl.multiple_of((zs + Z) % Z * rows, rows), rows), :]

    def pass_on(o):
        ref = block(z - o)
        if o != 0:
            wait(ref, w_recv.at[o % Z])
        for c in kids.get(o, ()):
            remote(w_hbm if o == 0 else ref, ref, w_send, w_recv.at[c % Z], dev(x, z + c - o))

    pass_on(0)
    for s in (1, 3, 2):
        remote(og_hbm, mine_og, og_send, og_recv.at[x], dev(x + s, z))

    loads[0].wait()
    loads[1].wait()
    for j in range(LT):
        lanes = slice(j * SUB, (j + 1) * SUB)
        ext[j, tok:, :] = (k[:, lanes].astype(F32) * v[:, lanes].astype(F32)).astype(BF)

    @pl.when(ctx < C - 1)
    def _():
        remote(ext.at[:, pl.ds(tok, tok), :], ext.at[:, pl.ds(0, tok), :], p_send, p_recv, ((ctx + 1) % C, f))

    @pl.when(ctx == 0)
    def _():
        ext[:, 0:tok, :] = jnp.zeros((LT, tok, SUB), BF)

    loads[2].wait()
    taps = filt[...].astype(BF)
    i0 = lax.broadcasted_iota(jnp.int32, (SUB, 2 * SUB), 0)
    i1 = lax.broadcasted_iota(jnp.int32, (SUB, 2 * SUB), 1)

    def build(picks, band):
        base = jnp.dot(taps, jnp.where(picks, 1.0, 0.0).astype(BF), preferred_element_type=F32)
        for g in range(base.shape[0]):
            row = jnp.broadcast_to(base[g : g + 1, :], (SUB, 2 * SUB))
            band[g * SUB : (g + 1) * SUB, :] = pltpu.roll(row, 0, 1, stride=1, stride_axis=0).astype(BF)

    lane_group = lax.broadcasted_iota(jnp.int32, (tok, SUB), 1) // 16

    def apply(band, lo, hi, data, j):
        n = SUB // 16
        rows_j = pl.ds(pl.multiple_of(j * n * SUB, n * SUB), n * SUB)
        res = jnp.dot(band[rows_j, lo:hi], data, preferred_element_type=F32)
        out = res[0:SUB]
        for g in range(1, n):
            out = jnp.where(lane_group == g, res[g * SUB : (g + 1) * SUB], out)
        return out

    zg = z // per

    def dgate(group):
        group = (group + NG) % NG
        for i in range(per):
            zs = group * per + i
            o = (z - zs + Z) % Z

            leaf = o != 0
            for ld in lead:
                leaf = jnp.logical_and(leaf, o != ld % Z)

            @pl.when(leaf)
            def _():
                wait(block(zs), w_recv.at[o])

        at = pl.ds(pl.multiple_of(group * SUB, SUB), SUB)
        part = lax.dot_general(
            og[...], w[at, :], (((1,), (1,)), ((), ())), preferred_element_type=F32
        ).astype(BF)
        base = x * line + group * SUB
        owner, lane = base // chans, base % chans // SUB
        for xx in range(X):
            mine = jnp.logical_and(xx == x, owner == f)
            piece = part[xx * tok : (xx + 1) * tok, :]

            @pl.when(mine)
            def _():
                recv[f, lane, :, :] = piece

            @pl.when(jnp.logical_not(mine))
            def _():
                stage[group, xx, :, :] = piece
                remote(stage.at[group, xx], recv.at[f, lane], r_send, r_recv.at[f, lane], dev(xx, z, owner))

    def dgates(first, count, step=1):
        def body(i, c):
            dgate(zg + first + i * step)
            return c

        lax.fori_loop(0, count, body, 0)

    def gated_slot(xx, h):
        return gated.at[pl.ds(pl.multiple_of(xx * tok, tok), tok), pl.ds(pl.multiple_of(h * chans, chans), chans)]

    def along_x():
        for t in (2, 1, 3):
            y0 = (x + t) % X

            @pl.when(y0 != y)
            def _():
                wait(gpass.at[y0], gp_recv.at[y0])
                remote(gpass.at[y0], gated_slot(x, core), g_send, gx_recv.at[x], dev(y0, z))

    def to_twin():
        for t in range(X):
            x0 = (x + t) % X
            ref = gated_slot(x0, core)
            if t == 0:
                @pl.when(home)
                def _():
                    wait(ref, g_self)

                @pl.when(jnp.logical_not(home))
                def _():
                    wait(ref, gp_recv.at[x])
            else:
                wait(ref, gx_recv.at[x0])
            remote(ref, ref, gt_send, gt_recv.at[x0], dev(x, z, twin))

    def forward_conv():
        @pl.when(ctx > 0)
        def _():
            wait(ext.at[:, pl.ds(0, tok), :], p_recv)

        loads[3].wait()
        for j in range(LT):
            lanes = slice(j * SUB, (j + 1) * SUB)
            cv = apply(band_f, 0, 2 * SUB, ext[j], j)
            conv[j, :, :] = cv
            g_own[:, lanes] = (q[:, lanes].astype(F32) * cv).astype(BF)
        for t in (2, 1, 3):
            who = dev(x, z, (f + HP * t) % NF)

            @pl.when(home)
            def _():
                remote(g_own, gated_slot(x, core), g_send, gp_recv.at[y], who)

            @pl.when(jnp.logical_not(home))
            def _():
                remote(g_own, gpass.at[y], g_send, gp_recv.at[y], who)

        @pl.when(home)
        def _():
            pltpu.make_async_copy(g_own, gated_slot(x, core), g_self).start()

        @pl.when(jnp.logical_not(home))
        def _():
            remote(g_own, gated_slot(x, core), g_send, gx_recv.at[x], dev(y, z))
        build(i0 == i1, band_b)

    def cotangents():
        own_w.wait()
        own_og.wait()
        for s in range(1, X):
            src = (x + s) % X
            wait(og.at[pl.ds(pl.multiple_of(src * tok, tok), tok), :], og_recv.at[src])

    build(i0 + i1 == SUB, band_f)
    stages = Z // 2 // STRIDE
    half = NG // 2
    ready = 0
    for m in range(1, stages + 1):
        for o in lead:
            if (m - 1) * STRIDE < abs(o) <= m * STRIDE:
                pass_on(o)
        if m == min(CONV_AT, stages):
            forward_conv()
        if m == min(OG_AT, stages):
            cotangents()
        if m == min(X_AT, stages):
            along_x()
        reach = [o for o in parent if abs(parent[o]) > (m - 1) * STRIDE]
        reach = min(abs(o) for o in reach) if reach else Z
        while m >= OG_AT and ready < half and per * ready + per - 1 < reach and m < stages:
            dgates(ready, 1 if ready == 0 else 2, -2 * ready)
            ready += 1
    if 0 < ready < half - 1:
        dgates(ready, 2, -2 * ready)
        ready += 1
    to_twin()
    for r in range(ready, half):
        dgates(r, 1 if r == 0 else 2, -2 * r)
    dgates(half, 1)

    for xx in range(X):
        wait(gated_slot(xx, (core + 1) % HP), gt_recv.at[xx])

    for s in (2, 1, 3, 0):
        xx = (x + s) % X
        part = jnp.dot(
            gated[pl.ds(pl.multiple_of(xx * tok, tok), tok), :], w[...], preferred_element_type=F32
        )
        if s == 0:
            mix_f[...] = part
        else:
            mstage[s, :, :] = part.astype(BF)
            remote(mstage.at[s], mrecv.at[x], m_send, m_recv.at[x], dev(xx, z))

    def gate_grad(j):
        total = jnp.zeros((tok, SUB), F32)
        for s in range(NF):
            src = (f + s) % NF
            if s == 0:
                @pl.when(jnp.logical_not(home))
                def _():
                    wait(recv.at[src, j], r_recv.at[src, j])
            else:
                wait(recv.at[src, j], r_recv.at[src, j])
            total = total + recv[src, j, :, :].astype(F32)
        lanes = pl.ds(pl.multiple_of(j * SUB, SUB), SUB)
        cg[j, :, :] = (total * q[:, lanes].astype(F32)).astype(BF)
        qg_o[:, lanes] = (total * conv[j, :, :]).astype(BF)

        @pl.when(ctx > 0)
        def _():
            remote(cg.at[j], nxt.at[j], c_send.at[j], c_recv.at[j], ((ctx + C - 1) % C, f))

    def at_distance(dist, c):
        def lane(j, cc):
            ahead = (core * LT + j - zg + NG) % NG

            @pl.when(jnp.minimum(ahead, (NG - ahead) % NG) == dist)
            def _():
                gate_grad(j)

            return cc

        return lax.fori_loop(0, LT, lane, c)

    lax.fori_loop(0, half + 1, at_distance, 0)
    for j in range(LT):
        conv[j, :, :] = apply(band_b, 0, SUB, cg[j], j)

    mix = mix_f[...]
    for s in range(1, X):
        src = (x + s) % X
        wait(mrecv.at[src], m_recv.at[src])
        mix = mix + mrecv[src, :, :].astype(F32)
    mix_o[...] = mix.astype(BF)

    @pl.when(ctx == C - 1)
    def _():
        nxt[...] = jnp.zeros_like(nxt)

    for j in range(LT):
        @pl.when(ctx < C - 1)
        def _():
            wait(nxt.at[j], c_recv.at[j])

        lanes = slice(j * SUB, (j + 1) * SUB)
        both = conv[j, :, :] + apply(band_b, SUB, 2 * SUB, nxt[j], j)
        kg_o[:, lanes] = (both * v[:, lanes].astype(F32)).astype(BF)
        vg_o[:, lanes] = (both * k[:, lanes].astype(F32)).astype(BF)

    wait(w.at[pl.ds(0, (Z - 1) * rows), :], w_send)
    wait(og.at[pl.ds(0, (X - 1) * tok), :], og_send)
    wait(mrecv.at[pl.ds(0, X - 1)], m_send)
    wait(gpass, gt_send)

    wait(recv.at[pl.ds(0, 2 * (X - 1))], g_send)

    @pl.when(home)
    def _():
        wait(recv.at[pl.ds(0, NF - 1)], r_send)

    @pl.when(jnp.logical_not(home))
    def _():
        wait(recv, r_send)

    @pl.when(ctx < C - 1)
    def _():
        wait(ext.at[:, pl.ds(0, tok), :], p_send)

    @pl.when(ctx > 0)
    def _():
        for j in range(LT):
            wait(cg.at[j], c_send.at[j])


def put_out(*refs):
    sem = refs[-1]
    n = len(refs) // 2
    copies = [pltpu.make_async_copy(refs[i], refs[n + i], sem.at[i]) for i in range(n)]
    for c in copies:
        c.start()
    for c in copies:
        c.wait()


def solution(mesh):
    NF = mesh.shape["fsdp"]
    X = X_CHIPS
    Z = mesh.shape["ctx"] // X

    def on_device(q, k, v, f, w, og):
        tok, ch = q.shape
        lt = ch // SUB
        rows, cols = w.shape
        line = Z * rows
        dma = pltpu.SemaphoreType.DMA
        res = pl.pallas_call(
            functools.partial(kernel, X, Z, NF),
            out_shape=[jax.ShapeDtypeStruct((tok, n), BF) for n in (cols, ch, ch, ch)],
            in_specs=[pl.BlockSpec(memory_space=pltpu.HBM)] * 6,
            out_specs=[pl.BlockSpec(memory_space=pltpu.VMEM)] * 4,
            scratch_shapes=[
                pltpu.VMEM((tok, ch), BF),
                pltpu.VMEM((tok, ch), BF),
                pltpu.VMEM((tok, ch), BF),
                pltpu.VMEM(f.shape, F32),
                pltpu.VMEM((line, cols), BF),
                pltpu.VMEM((X * tok, cols), BF),
                pltpu.VMEM((lt, 2 * tok, SUB), BF),
                pltpu.VMEM((f.shape[0] * SUB, 2 * SUB), BF),
                pltpu.VMEM((f.shape[0] * SUB, 2 * SUB), BF),
                pltpu.VMEM((lt, tok, SUB), F32),
                pltpu.VMEM((tok, ch), BF),
                pltpu.VMEM((X * tok, line), BF),
                pltpu.VMEM((X, tok, ch), BF),
                pltpu.VMEM((tok, cols), F32),
                pltpu.VMEM((line // SUB, X, tok, SUB), BF),
                pltpu.VMEM((NF, lt, tok, SUB), BF),
                pltpu.VMEM((lt, tok, SUB), BF),
                pltpu.VMEM((lt, tok, SUB), BF),
                pltpu.VMEM((X, tok, cols), BF),
                pltpu.VMEM((X, tok, cols), BF),
                dma((4,)), dma, dma((Z,)), dma, dma((X,)), dma, dma, dma((X,)), dma((X,)), dma, dma((X,)), dma,
                dma, dma((NF, lt)), dma, dma, dma((lt,)), dma((lt,)), dma, dma((X,)),
            ],
            compiler_params=pltpu.CompilerParams(
                collective_id=0, has_side_effects=True, vmem_limit_bytes=40 * 1024 * 1024
            ),
        )(*[pltpu.with_memory_space_constraint(a, pltpu.HBM) for a in (q, k, v, f, w, og)])
        n = len(res)
        return pl.pallas_call(
            put_out,
            out_shape=[jax.ShapeDtypeStruct(r.shape, r.dtype) for r in res],
            in_specs=[pl.BlockSpec(memory_space=pl.ANY)] * n,
            out_specs=[pl.BlockSpec(memory_space=pl.ANY)] * n,
            scratch_shapes=[dma((n,))],
            compiler_params=pltpu.CompilerParams(vmem_limit_bytes=1024 * 1024),
        )(*res)

    wide = P("ctx", "fsdp")
    return jax.shard_map(
        on_device,
        mesh=mesh,
        in_specs=(wide, wide, wide, P("fsdp", None), wide, wide),
        out_specs=(wide, wide, wide, wide),
        check_vma=False,
    )
```

```python
import functools

import jax
import jax.numpy as jnp
from jax import lax
from jax.experimental import pallas as pl
from jax.experimental.pallas import tpu as pltpu
from jax.sharding import PartitionSpec as P

MESH = pl.DeviceIdType.MESH
BF = jnp.bfloat16
F32 = jnp.float32
SUB = 128
X_CHIPS = 4
STRIDE = 4
CONV_AT, OG_AT, X_AT = 1, 2, 2


def broadcast_tree(size, stride):
    parent = {}
    for sgn in (1, -1):
        top = size // 2 if sgn == 1 else size // 2 - 1
        for o in range(1, top + 1):
            r = o % stride
            up = o - r + stride
            if r == 0:
                p = o - stride
            elif 2 * r > stride and up <= top:
                p = up
            elif r == 2 and stride == 4:
                p = o - 1
            else:
                p = o - r
            parent[sgn * o] = sgn * p
    kids = {}
    for o, p in parent.items():
        kids.setdefault(p, []).append(o)
    for p in kids:
        kids[p].sort(key=lambda o: -abs(o - p))
    return kids


def kernel(
    X, Z, NF,
    q_hbm, k_hbm, v_hbm, f_hbm, w_hbm, og_hbm,
    mix_o, qg_o, kg_o, vg_o,
    q, k, v, filt, w, og, ext, band_f, band_b, conv, g_own, gated, gpass, mix_f, stage, recv, cg, nxt, mstage, mrecv,
    load_sem, w_send, w_recv, og_send, og_recv, og_own, g_send, gp_recv, gx_recv, gt_send, gt_recv, g_self, r_send, r_recv,
    p_send, p_recv, c_send, c_recv, m_send, m_recv,
):
    C = X * Z
    rows, cols = w_hbm.shape
    tok, chans = q_hbm.shape
    LT = chans // SUB
    line = Z * rows
    HP = line // chans
    NG = line // SUB
    per = SUB // rows
    ctx = lax.axis_index("ctx")
    f = lax.axis_index("fsdp")
    x, z = ctx // Z, ctx % Z
    kids = broadcast_tree(Z, STRIDE)
    lead = sorted((o for o in kids if o), key=lambda o: (abs(o), -o))
    parent = {c: p for p in kids for c in kids[p]}

    def dev(xx, zz, ff=None):
        return (((xx + X) % X) * Z + (zz + Z) % Z, f if ff is None else ff)

    y, core = f // HP, f % HP
    twin = HP * y + (core + 1) % HP
    home = y == x
    barrier = pltpu.get_barrier_semaphore()
    jumps = sorted({o - p for p in kids for o in kids[p]} | {p - o for p in kids for o in kids[p]})
    partners = [dev(x, z + o) for o in jumps]
    partners += [dev(x + 1, z), dev(x - 1, z), dev(x + 2, z)]
    partners += [((ctx + 1) % C, f), ((ctx + C - 1) % C, f)]
    partners += [dev(x, z, (f + HP * t) % NF) for t in range(1, X)] + [dev(x, z, twin)]

    def hello(who):
        pl.semaphore_signal(barrier, inc=1, device_id=who, device_id_type=MESH)

    for who in partners:
        hello(who)
    for xx in range(X):
        for h in range(HP):
            ff = HP * x + h

            @pl.when(jnp.logical_or(xx != x, ff != f))
            def _():
                hello(dev(xx, z, ff))

    for ff in range(NF):
        @pl.when(jnp.logical_or(jnp.logical_not(home), ff != f))
        def _():
            hello(dev(f // HP, z, ff))

    loads = [(k_hbm, k), (v_hbm, v), (f_hbm, filt), (q_hbm, q)]
    loads = [pltpu.make_async_copy(a, b, load_sem.at[i]) for i, (a, b) in enumerate(loads)]
    mine_w = w.at[pl.ds(pl.multiple_of(z * rows, rows), rows), :]
    own_w = pltpu.make_async_copy(w_hbm, mine_w, w_recv.at[0])
    mine_og = og.at[pl.ds(pl.multiple_of(x * tok, tok), tok), :]
    own_og = pltpu.make_async_copy(og_hbm, mine_og, og_own)
    own_w.start()
    for c in loads:
        c.start()
    own_og.start()
    extra = X * HP + NF
    pl.semaphore_wait(barrier, len(partners) + jnp.where(home, extra - 2, extra))

    def remote(src, dst, ssem, rsem, who):
        pltpu.make_async_remote_copy(
            src_ref=src, dst_ref=dst, send_sem=ssem, recv_sem=rsem, device_id=who, device_id_type=MESH
        ).start()

    def wait(ref, sem):
        pltpu.make_async_copy(ref, ref, sem).wait()

    def block(zs):
        return w.at[pl.ds(pl.multiple_of((zs + Z) % Z * rows, rows), rows), :]

    def pass_on(o):
        ref = block(z - o)
        if o != 0:
            wait(ref, w_recv.at[o % Z])
        for c in kids.get(o, ()):
            remote(w_hbm if o == 0 else ref, ref, w_send, w_recv.at[c % Z], dev(x, z + c - o))

    pass_on(0)
    for s in (1, 3, 2):
        remote(og_hbm, mine_og, og_send, og_recv.at[x], dev(x + s, z))

    loads[0].wait()
    loads[1].wait()
    for j in range(LT):
        lanes = slice(j * SUB, (j + 1) * SUB)
        ext[j, tok:, :] = (k[:, lanes].astype(F32) * v[:, lanes].astype(F32)).astype(BF)

    @pl.when(ctx < C - 1)
    def _():
        remote(ext.at[:, pl.ds(tok, tok), :], ext.at[:, pl.ds(0, tok), :], p_send, p_recv, ((ctx + 1) % C, f))

    @pl.when(ctx == 0)
    def _():
        ext[:, 0:tok, :] = jnp.zeros((LT, tok, SUB), BF)

    loads[2].wait()
    taps = filt[...].astype(BF)
    i0 = lax.broadcasted_iota(jnp.int32, (SUB, 2 * SUB), 0)
    i1 = lax.broadcasted_iota(jnp.int32, (SUB, 2 * SUB), 1)

    def build(picks, band):
        base = jnp.dot(taps, jnp.where(picks, 1.0, 0.0).astype(BF), preferred_element_type=F32)
        for g in range(base.shape[0]):
            row = jnp.broadcast_to(base[g : g + 1, :], (SUB, 2 * SUB))
            band[g * SUB : (g + 1) * SUB, :] = pltpu.roll(row, 0, 1, stride=1, stride_axis=0).astype(BF)

    lane_group = lax.broadcasted_iota(jnp.int32, (tok, SUB), 1) // 16

    def apply(band, lo, hi, data, j):
        n = SUB // 16
        rows_j = pl.ds(pl.multiple_of(j * n * SUB, n * SUB), n * SUB)
        res = jnp.dot(band[rows_j, lo:hi], data, preferred_element_type=F32)
        out = res[0:SUB]
        for g in range(1, n):
            out = jnp.where(lane_group == g, res[g * SUB : (g + 1) * SUB], out)
        return out

    zg = z // per

    def dgate(group):
        group = (group + NG) % NG
        for i in range(per):
            zs = group * per + i
            o = (z - zs + Z) % Z

            leaf = o != 0
            for ld in lead:
                leaf = jnp.logical_and(leaf, o != ld % Z)

            @pl.when(leaf)
            def _():
                wait(block(zs), w_recv.at[o])

        at = pl.ds(pl.multiple_of(group * SUB, SUB), SUB)
        part = lax.dot_general(
            og[...], w[at, :], (((1,), (1,)), ((), ())), preferred_element_type=F32
        ).astype(BF)
        base = x * line + group * SUB
        owner, lane = base // chans, base % chans // SUB
        for xx in range(X):
            mine = jnp.logical_and(xx == x, owner == f)
            piece = part[xx * tok : (xx + 1) * tok, :]

            @pl.when(mine)
            def _():
                recv[f, lane, :, :] = piece

            @pl.when(jnp.logical_not(mine))
            def _():
                stage[group, xx, :, :] = piece
                remote(stage.at[group, xx], recv.at[f, lane], r_send, r_recv.at[f, lane], dev(xx, z, owner))

    def dgates(first, count, step=1):
        def body(i, c):
            dgate(zg + first + i * step)
            return c

        lax.fori_loop(0, count, body, 0)

    def gated_slot(xx, h):
        return gated.at[pl.ds(pl.multiple_of(xx * tok, tok), tok), pl.ds(pl.multiple_of(h * chans, chans), chans)]

    def along_x():
        for t in (2, 1, 3):
            y0 = (x + t) % X

            @pl.when(y0 != y)
            def _():
                wait(gpass.at[y0], gp_recv.at[y0])
                remote(gpass.at[y0], gated_slot(x, core), g_send, gx_recv.at[x], dev(y0, z))

    def to_twin():
        for t in range(X):
            x0 = (x + t) % X
            ref = gated_slot(x0, core)
            if t == 0:
                @pl.when(home)
                def _():
                    wait(ref, g_self)

                @pl.when(jnp.logical_not(home))
                def _():
                    wait(ref, gp_recv.at[x])
            else:
                wait(ref, gx_recv.at[x0])
            remote(ref, ref, gt_send, gt_recv.at[x0], dev(x, z, twin))

    def forward_conv():
        @pl.when(ctx > 0)
        def _():
            wait(ext.at[:, pl.ds(0, tok), :], p_recv)

        loads[3].wait()
        for j in range(LT):
            lanes = slice(j * SUB, (j + 1) * SUB)
            cv = apply(band_f, 0, 2 * SUB, ext[j], j)
            conv[j, :, :] = cv
            g_own[:, lanes] = (q[:, lanes].astype(F32) * cv).astype(BF)
        for t in (2, 1, 3):
            who = dev(x, z, (f + HP * t) % NF)

            @pl.when(home)
            def _():
                remote(g_own, gated_slot(x, core), g_send, gp_recv.at[y], who)

            @pl.when(jnp.logical_not(home))
            def _():
                remote(g_own, gpass.at[y], g_send, gp_recv.at[y], who)

        @pl.when(home)
        def _():
            pltpu.make_async_copy(g_own, gated_slot(x, core), g_self).start()

        @pl.when(jnp.logical_not(home))
        def _():
            remote(g_own, gated_slot(x, core), g_send, gx_recv.at[x], dev(y, z))
        build(i0 == i1, band_b)

    def cotangents():
        own_w.wait()
        own_og.wait()
        for s in range(1, X):
            src = (x + s) % X
            wait(og.at[pl.ds(pl.multiple_of(src * tok, tok), tok), :], og_recv.at[src])

    build(i0 + i1 == SUB, band_f)
    stages = Z // 2 // STRIDE
    half = NG // 2
    ready = 0
    for m in range(1, stages + 1):
        for o in lead:
            if (m - 1) * STRIDE < abs(o) <= m * STRIDE:
                if o == Z // 2 and 0 < ready < half - 1:
                    dgates(ready, 2, -2 * ready)
                    ready += 1
                pass_on(o)
        if m == min(CONV_AT, stages):
            forward_conv()
        if m == min(OG_AT, stages):
            cotangents()
        if m == min(X_AT, stages):
            along_x()
        reach = [o for o in parent if abs(parent[o]) > (m - 1) * STRIDE]
        reach = min(abs(o) for o in reach) if reach else Z
        while m >= OG_AT and ready < half and per * ready + per - 1 < reach and m < stages:
            dgates(ready, 1 if ready == 0 else 2, -2 * ready)
            ready += 1
    for r in range(ready, half):
        dgates(r, 1 if r == 0 else 2, -2 * r)
    dgates(half, 1)
    to_twin()

    for xx in range(X):
        wait(gated_slot(xx, (core + 1) % HP), gt_recv.at[xx])

    for s in (2, 1, 3, 0):
        xx = (x + s) % X
        part = jnp.dot(
            gated[pl.ds(pl.multiple_of(xx * tok, tok), tok), :], w[...], preferred_element_type=F32
        )
        if s == 0:
            mix_f[...] = part
        else:
            mstage[s, :, :] = part.astype(BF)
            remote(mstage.at[s], mrecv.at[x], m_send, m_recv.at[x], dev(xx, z))

    def gate_grad(j):
        total = jnp.zeros((tok, SUB), F32)
        for s in range(NF):
            src = (f + s) % NF
            if s == 0:
                @pl.when(jnp.logical_not(home))
                def _():
                    wait(recv.at[src, j], r_recv.at[src, j])
            else:
                wait(recv.at[src, j], r_recv.at[src, j])
            total = total + recv[src, j, :, :].astype(F32)
        lanes = pl.ds(pl.multiple_of(j * SUB, SUB), SUB)
        cg[j, :, :] = (total * q[:, lanes].astype(F32)).astype(BF)
        qg_o[:, lanes] = (total * conv[j, :, :]).astype(BF)

        @pl.when(ctx > 0)
        def _():
            remote(cg.at[j], nxt.at[j], c_send.at[j], c_recv.at[j], ((ctx + C - 1) % C, f))

    def at_distance(dist, c):
        def lane(j, cc):
            ahead = (core * LT + j - zg + NG) % NG

            @pl.when(jnp.minimum(ahead, (NG - ahead) % NG) == dist)
            def _():
                gate_grad(j)

            return cc

        return lax.fori_loop(0, LT, lane, c)

    lax.fori_loop(0, half + 1, at_distance, 0)
    for j in range(LT):
        conv[j, :, :] = apply(band_b, 0, SUB, cg[j], j)

    @pl.when(ctx == C - 1)
    def _():
        nxt[...] = jnp.zeros_like(nxt)

    for j in range(LT):
        @pl.when(ctx < C - 1)
        def _():
            wait(nxt.at[j], c_recv.at[j])

        lanes = slice(j * SUB, (j + 1) * SUB)
        both = conv[j, :, :] + apply(band_b, SUB, 2 * SUB, nxt[j], j)
        kg_o[:, lanes] = (both * v[:, lanes].astype(F32)).astype(BF)
        vg_o[:, lanes] = (both * k[:, lanes].astype(F32)).astype(BF)

    mix = mix_f[...]
    for s in range(1, X):
        src = (x + s) % X
        wait(mrecv.at[src], m_recv.at[src])
        mix = mix + mrecv[src, :, :].astype(F32)
    mix_o[...] = mix.astype(BF)

    wait(w.at[pl.ds(0, (Z - 1) * rows), :], w_send)
    wait(og.at[pl.ds(0, (X - 1) * tok), :], og_send)
    wait(mrecv.at[pl.ds(0, X - 1)], m_send)
    wait(gpass, gt_send)

    wait(recv.at[pl.ds(0, 2 * (X - 1))], g_send)

    @pl.when(home)
    def _():
        wait(recv.at[pl.ds(0, NF - 1)], r_send)

    @pl.when(jnp.logical_not(home))
    def _():
        wait(recv, r_send)

    @pl.when(ctx < C - 1)
    def _():
        wait(ext.at[:, pl.ds(0, tok), :], p_send)

    @pl.when(ctx > 0)
    def _():
        for j in range(LT):
            wait(cg.at[j], c_send.at[j])


def put_out(*refs):
    sem = refs[-1]
    n = len(refs) // 2
    copies = [pltpu.make_async_copy(refs[i], refs[n + i], sem.at[i]) for i in range(n)]
    for c in copies:
        c.start()
    for c in copies:
        c.wait()


def solution(mesh):
    NF = mesh.shape["fsdp"]
    X = X_CHIPS
    Z = mesh.shape["ctx"] // X

    def on_device(q, k, v, f, w, og):
        tok, ch = q.shape
        lt = ch // SUB
        rows, cols = w.shape
        line = Z * rows
        dma = pltpu.SemaphoreType.DMA
        res = pl.pallas_call(
            functools.partial(kernel, X, Z, NF),
            out_shape=[jax.ShapeDtypeStruct((tok, n), BF) for n in (cols, ch, ch, ch)],
            in_specs=[pl.BlockSpec(memory_space=pltpu.HBM)] * 6,
            out_specs=[pl.BlockSpec(memory_space=pltpu.VMEM)] * 4,
            scratch_shapes=[
                pltpu.VMEM((tok, ch), BF),
                pltpu.VMEM((tok, ch), BF),
                pltpu.VMEM((tok, ch), BF),
                pltpu.VMEM(f.shape, F32),
                pltpu.VMEM((line, cols), BF),
                pltpu.VMEM((X * tok, cols), BF),
                pltpu.VMEM((lt, 2 * tok, SUB), BF),
                pltpu.VMEM((f.shape[0] * SUB, 2 * SUB), BF),
                pltpu.VMEM((f.shape[0] * SUB, 2 * SUB), BF),
                pltpu.VMEM((lt, tok, SUB), F32),
                pltpu.VMEM((tok, ch), BF),
                pltpu.VMEM((X * tok, line), BF),
                pltpu.VMEM((X, tok, ch), BF),
                pltpu.VMEM((tok, cols), F32),
                pltpu.VMEM((line // SUB, X, tok, SUB), BF),
                pltpu.VMEM((NF, lt, tok, SUB), BF),
                pltpu.VMEM((lt, tok, SUB), BF),
                pltpu.VMEM((lt, tok, SUB), BF),
                pltpu.VMEM((X, tok, cols), BF),
                pltpu.VMEM((X, tok, cols), BF),
                dma((4,)), dma, dma((Z,)), dma, dma((X,)), dma, dma, dma((X,)), dma((X,)), dma, dma((X,)), dma,
                dma, dma((NF, lt)), dma, dma, dma((lt,)), dma((lt,)), dma, dma((X,)),
            ],
            compiler_params=pltpu.CompilerParams(
                collective_id=0, has_side_effects=True, vmem_limit_bytes=40 * 1024 * 1024
            ),
        )(*[pltpu.with_memory_space_constraint(a, pltpu.HBM) for a in (q, k, v, f, w, og)])
        n = len(res)
        return pl.pallas_call(
            put_out,
            out_shape=[jax.ShapeDtypeStruct(r.shape, r.dtype) for r in res],
            in_specs=[pl.BlockSpec(memory_space=pl.ANY)] * n,
            out_specs=[pl.BlockSpec(memory_space=pl.ANY)] * n,
            scratch_shapes=[dma((n,))],
            compiler_params=pltpu.CompilerParams(vmem_limit_bytes=1024 * 1024),
        )(*res)

    wide = P("ctx", "fsdp")
    return jax.shard_map(
        on_device,
        mesh=mesh,
        in_specs=(wide, wide, wide, P("fsdp", None), wide, wide),
        out_specs=(wide, wide, wide, wide),
        check_vma=False,
    )
```

```python
import functools

import jax
import jax.numpy as jnp
from jax import lax
from jax.experimental import pallas as pl
from jax.experimental.pallas import tpu as pltpu
from jax.sharding import PartitionSpec as P

MESH = pl.DeviceIdType.MESH
BF = jnp.bfloat16
F32 = jnp.float32
SUB = 128
X_CHIPS = 4
STRIDE = 4
CONV_AT, OG_AT, X_AT = 1, 2, 2


def broadcast_tree(size, stride):
    parent = {}
    for sgn in (1, -1):
        top = size // 2 if sgn == 1 else size // 2 - 1
        for o in range(1, top + 1):
            r = o % stride
            up = o - r + stride
            if r == 0:
                p = o - stride
            elif 2 * r > stride and up <= top:
                p = up
            elif r == 2 and stride == 4:
                p = o - 1
            else:
                p = o - r
            parent[sgn * o] = sgn * p
    kids = {}
    for o, p in parent.items():
        kids.setdefault(p, []).append(o)
    for p in kids:
        kids[p].sort(key=lambda o: -abs(o - p))
    return kids


def kernel(
    X, Z, NF,
    q_hbm, k_hbm, v_hbm, f_hbm, w_hbm, og_hbm,
    mix_o, qg_o, kg_o, vg_o,
    q, k, v, filt, w, og, ext, band_f, band_b, conv, g_own, gated, gpass, mix_f, stage, recv, cg, nxt, mstage, mrecv,
    load_sem, w_send, w_recv, og_send, og_recv, og_own, g_send, gp_recv, gx_recv, gt_send, gt_recv, g_self, r_send, r_recv,
    p_send, p_recv, c_send, c_recv, m_send, m_recv,
):
    C = X * Z
    rows, cols = w_hbm.shape
    tok, chans = q_hbm.shape
    LT = chans // SUB
    line = Z * rows
    HP = line // chans
    NG = line // SUB
    per = SUB // rows
    ctx = lax.axis_index("ctx")
    f = lax.axis_index("fsdp")
    x, z = ctx // Z, ctx % Z
    kids = broadcast_tree(Z, STRIDE)
    lead = sorted((o for o in kids if o), key=lambda o: (abs(o), -o))
    parent = {c: p for p in kids for c in kids[p]}

    def dev(xx, zz, ff=None):
        return (((xx + X) % X) * Z + (zz + Z) % Z, f if ff is None else ff)

    y, core = f // HP, f % HP
    twin = HP * y + (core + 1) % HP
    home = y == x
    barrier = pltpu.get_barrier_semaphore()
    jumps = sorted({o - p for p in kids for o in kids[p]} | {p - o for p in kids for o in kids[p]})
    partners = [dev(x, z + o) for o in jumps]
    partners += [dev(x + 1, z), dev(x - 1, z), dev(x + 2, z)]
    partners += [((ctx + 1) % C, f), ((ctx + C - 1) % C, f)]
    partners += [dev(x, z, (f + HP * t) % NF) for t in range(1, X)] + [dev(x, z, twin)]

    def hello(who):
        pl.semaphore_signal(barrier, inc=1, device_id=who, device_id_type=MESH)

    for who in partners:
        hello(who)
    for xx in range(X):
        for h in range(HP):
            ff = HP * x + h

            @pl.when(jnp.logical_or(xx != x, ff != f))
            def _():
                hello(dev(xx, z, ff))

    for ff in range(NF):
        @pl.when(jnp.logical_or(jnp.logical_not(home), ff != f))
        def _():
            hello(dev(f // HP, z, ff))

    loads = [(k_hbm, k), (v_hbm, v), (f_hbm, filt), (q_hbm, q)]
    loads = [pltpu.make_async_copy(a, b, load_sem.at[i]) for i, (a, b) in enumerate(loads)]
    mine_w = w.at[pl.ds(pl.multiple_of(z * rows, rows), rows), :]
    own_w = pltpu.make_async_copy(w_hbm, mine_w, w_recv.at[0])
    mine_og = og.at[pl.ds(pl.multiple_of(x * tok, tok), tok), :]
    own_og = pltpu.make_async_copy(og_hbm, mine_og, og_own)
    own_w.start()
    for c in loads:
        c.start()
    own_og.start()
    extra = X * HP + NF
    pl.semaphore_wait(barrier, len(partners) + jnp.where(home, extra - 2, extra))

    def remote(src, dst, ssem, rsem, who):
        pltpu.make_async_remote_copy(
            src_ref=src, dst_ref=dst, send_sem=ssem, recv_sem=rsem, device_id=who, device_id_type=MESH
        ).start()

    def wait(ref, sem):
        pltpu.make_async_copy(ref, ref, sem).wait()

    def block(zs):
        return w.at[pl.ds(pl.multiple_of((zs + Z) % Z * rows, rows), rows), :]

    def pass_on(o):
        ref = block(z - o)
        if o != 0:
            wait(ref, w_recv.at[o % Z])
        for c in kids.get(o, ()):
            remote(w_hbm if o == 0 else ref, ref, w_send, w_recv.at[c % Z], dev(x, z + c - o))

    pass_on(0)
    for s in (1, 3, 2):
        remote(og_hbm, mine_og, og_send, og_recv.at[x], dev(x + s, z))

    loads[0].wait()
    loads[1].wait()
    for j in range(LT):
        lanes = slice(j * SUB, (j + 1) * SUB)
        ext[j, tok:, :] = (k[:, lanes].astype(F32) * v[:, lanes].astype(F32)).astype(BF)

    @pl.when(ctx < C - 1)
    def _():
        remote(ext.at[:, pl.ds(tok, tok), :], ext.at[:, pl.ds(0, tok), :], p_send, p_recv, ((ctx + 1) % C, f))

    @pl.when(ctx == 0)
    def _():
        ext[:, 0:tok, :] = jnp.zeros((LT, tok, SUB), BF)

    loads[2].wait()
    taps = filt[...].astype(BF)
    i0 = lax.broadcasted_iota(jnp.int32, (SUB, 2 * SUB), 0)
    i1 = lax.broadcasted_iota(jnp.int32, (SUB, 2 * SUB), 1)

    def build(picks, band):
        base = jnp.dot(taps, jnp.where(picks, 1.0, 0.0).astype(BF), preferred_element_type=F32)
        for g in range(base.shape[0]):
            row = jnp.broadcast_to(base[g : g + 1, :], (SUB, 2 * SUB))
            band[g * SUB : (g + 1) * SUB, :] = pltpu.roll(row, 0, 1, stride=1, stride_axis=0).astype(BF)

    lane_group = lax.broadcasted_iota(jnp.int32, (tok, SUB), 1) // 16

    def apply(band, lo, hi, data, j):
        n = SUB // 16
        rows_j = pl.ds(pl.multiple_of(j * n * SUB, n * SUB), n * SUB)
        res = jnp.dot(band[rows_j, lo:hi], data, preferred_element_type=F32)
        out = res[0:SUB]
        for g in range(1, n):
            out = jnp.where(lane_group == g, res[g * SUB : (g + 1) * SUB], out)
        return out

    zg = z // per

    def dgate(group):
        group = (group + NG) % NG
        for i in range(per):
            zs = group * per + i
            o = (z - zs + Z) % Z

            leaf = o != 0
            for ld in lead:
                leaf = jnp.logical_and(leaf, o != ld % Z)

            @pl.when(leaf)
            def _():
                wait(block(zs), w_recv.at[o])

        at = pl.ds(pl.multiple_of(group * SUB, SUB), SUB)
        part = lax.dot_general(
            og[...], w[at, :], (((1,), (1,)), ((), ())), preferred_element_type=F32
        ).astype(BF)
        base = x * line + group * SUB
        owner, lane = base // chans, base % chans // SUB
        for xx in range(X):
            stage[group, xx, :, :] = part[xx * tok : (xx + 1) * tok, :]
        for s in (2, 1, 3):
            xx = (x + s) % X
            remote(stage.at[group, xx], recv.at[f, lane], r_send, r_recv.at[f, lane], dev(xx, z, owner))

        @pl.when(owner == f)
        def _():
            recv[f, lane, :, :] = stage[group, x, :, :]

        @pl.when(owner != f)
        def _():
            remote(stage.at[group, x], recv.at[f, lane], r_send, r_recv.at[f, lane], dev(x, z, owner))

    def dgates(first, count, step=1):
        def body(i, c):
            dgate(zg + first + i * step)
            return c

        lax.fori_loop(0, count, body, 0)

    def gated_slot(xx, h):
        return gated.at[pl.ds(pl.multiple_of(xx * tok, tok), tok), pl.ds(pl.multiple_of(h * chans, chans), chans)]

    def along_x():
        for t in (2, 1, 3):
            y0 = (x + t) % X

            @pl.when(y0 != y)
            def _():
                wait(gpass.at[y0], gp_recv.at[y0])
                remote(gpass.at[y0], gated_slot(x, core), g_send, gx_recv.at[x], dev(y0, z))

    def to_twin():
        for t in range(X):
            x0 = (x + t) % X
            ref = gated_slot(x0, core)
            if t == 0:
                @pl.when(home)
                def _():
                    wait(ref, g_self)

                @pl.when(jnp.logical_not(home))
                def _():
                    wait(ref, gp_recv.at[x])
            else:
                wait(ref, gx_recv.at[x0])
            remote(ref, ref, gt_send, gt_recv.at[x0], dev(x, z, twin))

    def forward_conv():
        @pl.when(ctx > 0)
        def _():
            wait(ext.at[:, pl.ds(0, tok), :], p_recv)

        loads[3].wait()
        for j in range(LT):
            lanes = slice(j * SUB, (j + 1) * SUB)
            cv = apply(band_f, 0, 2 * SUB, ext[j], j)
            conv[j, :, :] = cv
            g_own[:, lanes] = (q[:, lanes].astype(F32) * cv).astype(BF)
        for t in (2, 1, 3):
            who = dev(x, z, (f + HP * t) % NF)

            @pl.when(home)
            def _():
                remote(g_own, gated_slot(x, core), g_send, gp_recv.at[y], who)

            @pl.when(jnp.logical_not(home))
            def _():
                remote(g_own, gpass.at[y], g_send, gp_recv.at[y], who)

        @pl.when(home)
        def _():
            pltpu.make_async_copy(g_own, gated_slot(x, core), g_self).start()

        @pl.when(jnp.logical_not(home))
        def _():
            remote(g_own, gated_slot(x, core), g_send, gx_recv.at[x], dev(y, z))
        build(i0 == i1, band_b)

    def cotangents():
        own_w.wait()
        own_og.wait()
        for s in range(1, X):
            src = (x + s) % X
            wait(og.at[pl.ds(pl.multiple_of(src * tok, tok), tok), :], og_recv.at[src])

    build(i0 + i1 == SUB, band_f)
    stages = Z // 2 // STRIDE
    half = NG // 2
    ready = 0
    for m in range(1, stages + 1):
        for o in lead:
            if (m - 1) * STRIDE < abs(o) <= m * STRIDE:
                if o == Z // 2 and 0 < ready < half - 1:
                    dgates(ready, 2, -2 * ready)
                    ready += 1
                pass_on(o)
        if m == min(CONV_AT, stages):
            forward_conv()
        if m == min(OG_AT, stages):
            cotangents()
        if m == min(X_AT, stages):
            along_x()
        reach = [o for o in parent if abs(parent[o]) > (m - 1) * STRIDE]
        reach = min(abs(o) for o in reach) if reach else Z
        while m >= OG_AT and ready < half and per * ready + per - 1 < reach and m < stages:
            dgates(ready, 1 if ready == 0 else 2, -2 * ready)
            ready += 1
    for r in range(ready, half):
        dgates(r, 1 if r == 0 else 2, -2 * r)
    dgates(half, 1)
    to_twin()

    for xx in range(X):
        wait(gated_slot(xx, (core + 1) % HP), gt_recv.at[xx])

    for s in (2, 1, 3, 0):
        xx = (x + s) % X
        part = jnp.dot(
            gated[pl.ds(pl.multiple_of(xx * tok, tok), tok), :], w[...], preferred_element_type=F32
        )
        if s == 0:
            mix_f[...] = part
        else:
            mstage[s, :, :] = part.astype(BF)
            remote(mstage.at[s], mrecv.at[x], m_send, m_recv.at[x], dev(xx, z))

    def gate_grad(j):
        total = jnp.zeros((tok, SUB), F32)
        for s in range(NF):
            src = (f + s) % NF
            if s == 0:
                @pl.when(jnp.logical_not(home))
                def _():
                    wait(recv.at[src, j], r_recv.at[src, j])
            else:
                wait(recv.at[src, j], r_recv.at[src, j])
            total = total + recv[src, j, :, :].astype(F32)
        lanes = pl.ds(pl.multiple_of(j * SUB, SUB), SUB)
        cg[j, :, :] = (total * q[:, lanes].astype(F32)).astype(BF)
        qg_o[:, lanes] = (total * conv[j, :, :]).astype(BF)

        @pl.when(ctx > 0)
        def _():
            remote(cg.at[j], nxt.at[j], c_send.at[j], c_recv.at[j], ((ctx + C - 1) % C, f))

    def at_distance(dist, c):
        def lane(j, cc):
            ahead = (core * LT + j - zg + NG) % NG

            @pl.when(jnp.minimum(ahead, (NG - ahead) % NG) == dist)
            def _():
                gate_grad(j)

            return cc

        return lax.fori_loop(0, LT, lane, c)

    lax.fori_loop(0, half + 1, at_distance, 0)
    for j in range(LT):
        conv[j, :, :] = apply(band_b, 0, SUB, cg[j], j)

    @pl.when(ctx == C - 1)
    def _():
        nxt[...] = jnp.zeros_like(nxt)

    for j in range(LT):
        @pl.when(ctx < C - 1)
        def _():
            wait(nxt.at[j], c_recv.at[j])

        lanes = slice(j * SUB, (j + 1) * SUB)
        both = conv[j, :, :] + apply(band_b, SUB, 2 * SUB, nxt[j], j)
        kg_o[:, lanes] = (both * v[:, lanes].astype(F32)).astype(BF)
        vg_o[:, lanes] = (both * k[:, lanes].astype(F32)).astype(BF)

    mix = mix_f[...]
    for s in range(1, X):
        src = (x + s) % X
        wait(mrecv.at[src], m_recv.at[src])
        mix = mix + mrecv[src, :, :].astype(F32)
    mix_o[...] = mix.astype(BF)

    wait(w.at[pl.ds(0, (Z - 1) * rows), :], w_send)
    wait(og.at[pl.ds(0, (X - 1) * tok), :], og_send)
    wait(mrecv.at[pl.ds(0, X - 1)], m_send)
    wait(gpass, gt_send)

    wait(recv.at[pl.ds(0, 2 * (X - 1))], g_send)

    @pl.when(home)
    def _():
        wait(recv.at[pl.ds(0, NF - 1)], r_send)

    @pl.when(jnp.logical_not(home))
    def _():
        wait(recv, r_send)

    @pl.when(ctx < C - 1)
    def _():
        wait(ext.at[:, pl.ds(0, tok), :], p_send)

    @pl.when(ctx > 0)
    def _():
        for j in range(LT):
            wait(cg.at[j], c_send.at[j])


def put_out(*refs):
    sem = refs[-1]
    n = len(refs) // 2
    copies = [pltpu.make_async_copy(refs[i], refs[n + i], sem.at[i]) for i in range(n)]
    for c in copies:
        c.start()
    for c in copies:
        c.wait()


def solution(mesh):
    NF = mesh.shape["fsdp"]
    X = X_CHIPS
    Z = mesh.shape["ctx"] // X

    def on_device(q, k, v, f, w, og):
        tok, ch = q.shape
        lt = ch // SUB
        rows, cols = w.shape
        line = Z * rows
        dma = pltpu.SemaphoreType.DMA
        res = pl.pallas_call(
            functools.partial(kernel, X, Z, NF),
            out_shape=[jax.ShapeDtypeStruct((tok, n), BF) for n in (cols, ch, ch, ch)],
            in_specs=[pl.BlockSpec(memory_space=pltpu.HBM)] * 6,
            out_specs=[pl.BlockSpec(memory_space=pltpu.VMEM)] * 4,
            scratch_shapes=[
                pltpu.VMEM((tok, ch), BF),
                pltpu.VMEM((tok, ch), BF),
                pltpu.VMEM((tok, ch), BF),
                pltpu.VMEM(f.shape, F32),
                pltpu.VMEM((line, cols), BF),
                pltpu.VMEM((X * tok, cols), BF),
                pltpu.VMEM((lt, 2 * tok, SUB), BF),
                pltpu.VMEM((f.shape[0] * SUB, 2 * SUB), BF),
                pltpu.VMEM((f.shape[0] * SUB, 2 * SUB), BF),
                pltpu.VMEM((lt, tok, SUB), F32),
                pltpu.VMEM((tok, ch), BF),
                pltpu.VMEM((X * tok, line), BF),
                pltpu.VMEM((X, tok, ch), BF),
                pltpu.VMEM((tok, cols), F32),
                pltpu.VMEM((line // SUB, X, tok, SUB), BF),
                pltpu.VMEM((NF, lt, tok, SUB), BF),
                pltpu.VMEM((lt, tok, SUB), BF),
                pltpu.VMEM((lt, tok, SUB), BF),
                pltpu.VMEM((X, tok, cols), BF),
                pltpu.VMEM((X, tok, cols), BF),
                dma((4,)), dma, dma((Z,)), dma, dma((X,)), dma, dma, dma((X,)), dma((X,)), dma, dma((X,)), dma,
                dma, dma((NF, lt)), dma, dma, dma((lt,)), dma((lt,)), dma, dma((X,)),
            ],
            compiler_params=pltpu.CompilerParams(
                collective_id=0, has_side_effects=True, vmem_limit_bytes=40 * 1024 * 1024
            ),
        )(*[pltpu.with_memory_space_constraint(a, pltpu.HBM) for a in (q, k, v, f, w, og)])
        n = len(res)
        return pl.pallas_call(
            put_out,
            out_shape=[jax.ShapeDtypeStruct(r.shape, r.dtype) for r in res],
            in_specs=[pl.BlockSpec(memory_space=pl.ANY)] * n,
            out_specs=[pl.BlockSpec(memory_space=pl.ANY)] * n,
            scratch_shapes=[dma((n,))],
            compiler_params=pltpu.CompilerParams(vmem_limit_bytes=1024 * 1024),
        )(*res)

    wide = P("ctx", "fsdp")
    return jax.shard_map(
        on_device,
        mesh=mesh,
        in_specs=(wide, wide, wide, P("fsdp", None), wide, wide),
        out_specs=(wide, wide, wide, wide),
        check_vma=False,
    )
```
